32 devices in a mesh: batch: 4 (over y, x), corpus: 8 (over z, core).
Axes of the slice: x: 2, y: 2, z: 4, core: 2. Of those that a mesh axis runs over, the one named last changes fastest.
Arguments:
- states: bfloat16 [4096, 4096], P('batch', 'corpus'), may hold values from -6 to 6
- norm_gain: float32 [4096], replicated, may hold values from 0.25 to 1.75
- gate_weight: bfloat16 [4096, 12288], P('batch', 'corpus'), may hold values from -0.09375 to 0.09375
- up_weight: bfloat16 [4096, 12288], P('batch', 'corpus'), may hold values from -0.09375 to 0.09375
- down_weight: bfloat16 [12288, 4096], P('corpus', 'batch'), may hold values from -0.0546875 to 0.0546875
- final_gain: float32 [4096], replicated, may hold values from 0.25 to 1.75
- hash_weight: bfloat16 [4096, 1024], replicated, may hold values from -0.75 to 0.75
- query_bits: bfloat16 [4096, 1024], replicated, may hold values from -1 to 1
- slot_map: int32 [64], replicated, may hold values from 0 to 63, each once
- query_index: int32 [4096, 100], replicated, may hold values from 0 to 63
Outputs:
- scores: float32 [4096, 100], P(('batch', 'corpus'))
The draws below stay inside these ranges and needn't reach their ends.
Inputs may be any that keep to these rules, and one draw needn't show every extreme that they name: `slot_map`: each corpus entry is named by exactly one document.
All inputs are finite; a program needn't handle non-finite values.
Results may differ from the reference program's by a relative error of at most 0.017.
Values may be sent and summed in bfloat16 or wider, within the bound.
A program may use at most 192 MiB of HBM per device.

```python
import jax
import jax.numpy as jnp
from jax import lax

D = 4096
FF = 12288
DOC_LEN = 64
CODE = 1024
NQ = 4096
TOPK = 100
NDOC = 64
TOKENS = 4096
N_CORPUS = 8


def draw_query_bits(key, part):
    picks = jax.random.randint(jax.random.fold_in(key, 7), (NQ, CODE), 0, 2)
    return (2.0 * picks.astype(jnp.float32) - 1.0).astype(jnp.bfloat16)


def plant(entries, stream_key, low, high):
    longest = entries.shape.index(max(entries.shape))
    spots = []
    for shift in (0, 1):
        where = [jax.random.randint(jax.random.fold_in(stream_key, axis), (), 0, length) for axis, length in enumerate(entries.shape)]
        where[longest] = (where[longest] + shift) % entries.shape[longest]
        spots.append(tuple(where))
    return entries.at[spots[0]].set(low).at[spots[1]].set(high)


def steps_of(own_key, shape, cuts, low, largest):
    def one(position, shards_of):
        heights = jax.random.uniform(jax.random.fold_in(jax.random.fold_in(own_key, 6), position), (shards_of,), jnp.float32, low / len(cuts), largest / len(cuts))
        return jnp.repeat(jnp.exp(heights), shape[position] // shards_of).reshape((-1,) + (1,) * (len(shape) - position - 1))

    level = one(*cuts[0])
    for cut in cuts[1:]:
        level = level * one(*cut)
    return level


def scatter_about(stream_key, dims, scale, reach, pieces=(), dtype=jnp.bfloat16):
    result = jax.random.normal(stream_key, dims, jnp.float32) * scale
    if len(pieces) > 0:
        result = steps_of(stream_key, dims, pieces, -0.22, 0.18) * result
    return jnp.clip(result, min=-reach, max=reach).astype(dtype)


def setup_inputs(seed: int = 0) -> dict:
    key_list = jax.random.split(jax.random.key(seed), 11)
    return {
        "states": scatter_about(key_list[0], (TOKENS, D), 1.0, 6.0, ((0, 4), (1, 8))),
        "norm_gain": jnp.clip(1.0 + 0.15 * jax.random.normal(key_list[1], (D,), jnp.float32), 0.25, 1.75),
        "gate_weight": scatter_about(key_list[2], (D, FF), D ** -0.5, 0.09375, ((0, 4), (1, 8))),
        "up_weight": scatter_about(key_list[3], (D, FF), D ** -0.5, 0.09375, ((0, 4), (1, 8))),
        "down_weight": scatter_about(key_list[4], (FF, D), FF ** -0.5, 0.0546875, ((0, 8), (1, 4))),
        "final_gain": jnp.clip(1.0 + 0.15 * jax.random.normal(key_list[5], (D,), jnp.float32), 0.25, 1.75),
        "hash_weight": scatter_about(key_list[6], (D, CODE), (D // 64) ** -0.5, 0.75),
        "query_bits": draw_query_bits(jax.random.fold_in(key_list[10], 71), 0),
        "slot_map": jax.random.permutation(key_list[8], NDOC).astype(jnp.int32),
        "query_index": plant(jax.random.randint(key_list[9], (NQ, TOPK), 0, NDOC), jax.random.fold_in(key_list[9], 1), 0, NDOC - 1).astype(jnp.int32),
    }


def rms(values, gain):
    return values * lax.rsqrt(lax.optimization_barrier(jnp.mean(values * values, axis=-1, keepdims=True)) + 1e-06) * gain

def reference(states, norm_gain, gate_weight, up_weight, down_weight, final_gain, hash_weight, query_bits, slot_map, query_index):
    floats = states.astype(jnp.float32)
    normed = rms(floats, norm_gain).astype(jnp.bfloat16)
    gate = jnp.dot(normed, gate_weight, preferred_element_type=jnp.float32)
    up = jnp.dot(normed, up_weight, preferred_element_type=jnp.float32)
    hidden = (jax.nn.silu(gate) * up).astype(jnp.bfloat16)
    width = FF // N_CORPUS
    hidden_groups = hidden.reshape(TOKENS, N_CORPUS, width).transpose(1, 0, 2)
    down_groups = down_weight.reshape(N_CORPUS, width, D)

    def add_group(total, pair):
        part = jnp.dot(pair[0], pair[1], preferred_element_type=jnp.float32).astype(jnp.bfloat16)
        return (total + part.astype(jnp.float32), None)
    ffn, unused = lax.scan(add_group, jnp.zeros((TOKENS, D), jnp.float32), (hidden_groups, down_groups))
    resid = floats + ffn
    finals = rms(resid, final_gain)
    pooled = lax.optimization_barrier(jnp.mean(finals.reshape(NDOC, DOC_LEN, D), axis=1)).astype(jnp.bfloat16)
    codes = jnp.tanh(jnp.dot(pooled, hash_weight, preferred_element_type=jnp.float32)).astype(jnp.bfloat16)
    corpus = jnp.zeros((NDOC, CODE), jnp.bfloat16).at[slot_map].set(codes)
    table = jnp.dot(query_bits, corpus.T, preferred_element_type=jnp.float32) / jnp.sqrt(jnp.float32(CODE))
    return jnp.take_along_axis(table, query_index, axis=1)
```

```python
import jax
import jax.numpy as jnp
from jax import lax
from jax.experimental import pallas as pl
from jax.experimental.pallas import tpu as pltpu
from jax.sharding import PartitionSpec as P

DOC_LEN = 64


def rms(values, gain):
    return values * lax.rsqrt(jnp.mean(values * values, axis=-1, keepdims=True) + 1e-06) * gain


def add_rows(left, piece):
    return jnp.dot(left, piece, preferred_element_type=jnp.float32)


def score_kernel(place_ref, bits_ref, codes_ref, slot_ref, index_ref, out_ref, picks):
    docs = slot_ref.shape[1]
    lanes = picks.shape[0]
    top = index_ref.shape[0]
    if len(codes_ref.shape) == 3:
        chips, packed, width = codes_ref.shape
        groups = bits_ref.shape[1] // width
        each = packed // groups
        every = codes_ref[...].astype(jnp.float32)
        codes = jnp.concatenate(
            [
                jnp.concatenate(
                    [every[n, g * each : (g + 1) * each] for n in range(chips)], axis=0
                )
                for g in range(groups)
            ],
            axis=1,
        ).astype(jnp.bfloat16)
    else:
        codes = codes_ref[...]
    entry = lax.broadcasted_iota(jnp.int32, (lanes, docs), 0)
    placing = jnp.where(entry == slot_ref[...], 1.0, 0.0).astype(jnp.bfloat16)
    corpus = jnp.dot(placing, codes, preferred_element_type=jnp.float32).astype(jnp.bfloat16)
    table = lax.dot_general(
        bits_ref[...],
        corpus,
        (((1,), (1,)), ((), ())),
        preferred_element_type=jnp.float32,
    ) * (1.0 / float(bits_ref.shape[1]) ** 0.5)
    picks[...] = jnp.zeros_like(picks)
    picks[:top, :] = index_ref[...]
    out_ref[...] = jnp.take_along_axis(table, picks[...].T, axis=1).T[:top, :]


def score(query_bits, codes, slot_map, query_index, flat_index, rows):
    docs = slot_map.shape[0]
    bits = query_bits.shape[1]
    top = query_index.shape[1]
    lanes = 128 * max(pl.cdiv(docs, 128), pl.cdiv(top, 128))
    index = query_index.T
    if rows % 128 == 0:
        index_spec = pl.BlockSpec((top, rows), lambda i, f: (0, f[0]))
    else:
        index = lax.dynamic_slice_in_dim(index, flat_index * rows, rows, 1)
        index_spec = pl.BlockSpec((top, rows), lambda i, f: (0, 0))
    out = pl.pallas_call(
        score_kernel,
        out_shape=jax.ShapeDtypeStruct((top, rows), jnp.float32),
        grid_spec=pltpu.PrefetchScalarGridSpec(
            num_scalar_prefetch=1,
            grid=(1,),
            in_specs=[
                pl.BlockSpec((rows, bits), lambda i, f: (f[0], 0)),
                pl.BlockSpec(codes.shape, lambda i, f: (0,) * codes.ndim),
                pl.BlockSpec((1, docs), lambda i, f: (0, 0)),
                index_spec,
            ],
            out_specs=pl.BlockSpec((top, rows), lambda i, f: (0, 0)),
            scratch_shapes=[pltpu.VMEM((lanes, rows), jnp.int32)],
        ),
    )(flat_index.reshape(1), query_bits, codes, slot_map[None], index)
    return out.T


def wide_kernel(
    states_ref, gain_ref, gate_ref, up_ref, down_ref, last_ref, hash_ref, out_ref,
    X, G, U, W, AG, AU, H, SR, YR, ZR, R, SQ, PT, CA,
    s_loc, s_y, s_zr, s_zl, s_sib, w_loc, w_x, w_y, w_r, c_sib, c_y, c_z,
    h_sem, q_sem, p_sem, a_send, a_recv,
):
    nz = lax.axis_size("corpus") // 2
    b = lax.axis_index("batch")
    c = lax.axis_index("corpus")
    y, x = b // 2, b % 2
    z, k = c // 2, c % 2
    rows, feat = states_ref.shape
    half = W.shape[0]
    full = X.shape[1]
    cols = down_ref.shape[1]
    w = cols // 2
    by, bx, bd = (1 - y) * 2 + x, y * 2 + (1 - x), (1 - y) * 2 + (1 - x)
    to_y = {"batch": by}
    to_x = {"batch": bx}
    to_sib = {"corpus": z * 2 + (1 - k)}

    def at_z(other):
        return {"corpus": other * 2 + k}

    def remote(src, dst, sems, place):
        return pltpu.make_async_remote_copy(
            src_ref=src, dst_ref=dst, send_sem=sems.at[0], recv_sem=sems.at[1],
            device_id=place, device_id_type=pl.DeviceIdType.MESH,
        )

    def spot(t, zs, ks):
        block = y if t == 0 else 1 - y
        return X.at[
            pl.ds(pl.multiple_of(block * rows, rows), rows),
            pl.ds(pl.multiple_of((zs * 2 + ks) * feat, feat), feat),
        ]

    own_states = pltpu.make_async_copy(states_ref, spot(0, z, k), s_loc)
    y_states = remote(states_ref, X.at[
        pl.ds(pl.multiple_of(y * rows, rows), rows),
        pl.ds(pl.multiple_of(c * feat, feat), feat),
    ], s_y, to_y)

    def right(t, s):
        src = states_ref if t == 0 and s == 0 else spot(t, z - s, k)
        return remote(src, spot(t, z - s, k), s_zr.at[t, s], at_z(z + 1))

    def left(t, s):
        src = states_ref if t == 0 and s == 0 else spot(t, z + s, k)
        return remote(src, spot(t, z + s, k), s_zl.at[t, s], at_z(z - 1))

    def sib(t, zs):
        return remote(spot(t, zs, k), spot(t, zs, k), s_sib.at[t, zs], to_sib)

    def sib_in(t, zs):
        return remote(spot(t, zs, 1 - k), spot(t, zs, 1 - k), s_sib.at[t, zs], to_sib)

    def first(t):
        @pl.when(z + 1 < nz)
        def _():
            right(t, 0).start()

        @pl.when(z >= 1)
        def _():
            left(t, 0).start()

        sib(t, z).start()

    def relay(t, s):
        @pl.when(z - 1 - s >= 0)
        def _():
            right(t, s).wait_recv()
            if s + 1 < nz - 1:
                @pl.when(z + 1 < nz)
                def _():
                    right(t, s + 1).start()
            sib(t, z - 1 - s).start()

        @pl.when(z + 1 + s < nz)
        def _():
            left(t, s).wait_recv()
            if s + 1 < nz - 1:
                @pl.when(z >= 1)
                def _():
                    left(t, s + 1).start()
            sib(t, z + 1 + s).start()

    def part(m, mine):
        h = pl.ds(pl.multiple_of((y if mine else 1 - y) * half, half), half)
        if m == 2:
            return down_ref.at[h, :]
        return (gate_ref, up_ref)[m].at[:, h]

    def place(m, block):
        if m == 2:
            return W.at[:, pl.ds(pl.multiple_of(block * cols, cols), cols)]
        return (G, U)[m].at[pl.ds(pl.multiple_of(block * rows_w, rows_w), rows_w), :]

    rows_w = gate_ref.shape[0]
    loc = [pltpu.make_async_copy(part(m, True), place(m, b), w_loc.at[m]) for m in range(3)]
    wx = [remote(part(m, True), place(m, b), w_x.at[m], to_x) for m in range(3)]
    wy = [remote(part(m, False), place(m, b), w_y.at[m], to_y) for m in range(3)]
    wr = [remote(place(m, by), place(m, by), w_r.at[m], to_x) for m in range(3)]

    def settle(t):
        for zs in range(nz):
            sib_in(t, zs).wait_recv()
            sib(t, zs).wait_send()
        for s in range(nz - 1):
            @pl.when((z - s >= 0) & (z + 1 < nz))
            def _():
                right(t, s).wait_send()

            @pl.when((z + s < nz) & (z >= 1))
            def _():
                left(t, s).wait_send()

    gain = gain_ref[...]
    strip = min(512, rows)
    tile = min(256, rows)
    step = half // 3 if half % 384 == 0 else 128
    blocks = [x, 2 + x, 1 - x, 2 + (1 - x)]
    own_rows = R.shape[0]

    def norm(t):
        start = (y if t == 0 else 1 - y) * rows

        @pl.loop(0, rows // 32)
        def _(p):
            r = pl.ds(pl.multiple_of(start + p * 32, 32), 32)
            v = X[r, :].astype(jnp.float32)
            scale = lax.rsqrt(jnp.mean(v * v, axis=-1, keepdims=True) + 1e-06)
            X[r, :] = (v * scale * gain).astype(jnp.bfloat16)

    def block_product(block, order):
        depth = pl.ds(pl.multiple_of(block * rows_w, rows_w), rows_w)

        @pl.loop(0, rows // strip)
        def _(i):
            here = pl.ds(pl.multiple_of(i * strip, strip), strip)
            r = pl.ds(pl.multiple_of((1 - y) * rows + i * strip, strip), strip)

            @pl.loop(0, half // step)
            def _(j):
                h = pl.ds(pl.multiple_of(j * step, 128), step)
                g = jnp.dot(X[r, depth], G[depth, h], preferred_element_type=jnp.float32)
                u = jnp.dot(X[r, depth], U[depth, h], preferred_element_type=jnp.float32)
                if order > 0:
                    g = g + AG[here, h]
                    u = u + AU[here, h]
                if order < 3:
                    AG[here, h] = g
                    AU[here, h] = u
                else:
                    H[r, h] = (g * jax.nn.sigmoid(g) * u).astype(jnp.bfloat16)

    def own_product(low, high):
        @pl.loop(low, high)
        def _(i):
            r = pl.ds(pl.multiple_of(y * rows + i * tile, tile), tile)

            @pl.loop(0, half // step)
            def _(j):
                h = pl.ds(pl.multiple_of(j * step, 128), step)
                g = jnp.dot(X[r, :], G[:, h], preferred_element_type=jnp.float32)
                u = jnp.dot(X[r, :], U[:, h], preferred_element_type=jnp.float32)
                H[r, h] = (g * jax.nn.sigmoid(g) * u).astype(jnp.bfloat16)

    barrier = pltpu.get_barrier_semaphore()

    def greet(place):
        pl.semaphore_signal(
            barrier, inc=1, device_id=place, device_id_type=pl.DeviceIdType.MESH
        )

    greet(to_y)
    greet(to_x)
    greet(to_sib)

    @pl.when(z + 1 < nz)
    def _():
        greet(at_z(z + 1))

    @pl.when(z >= 1)
    def _():
        greet(at_z(z - 1))

    ends = jnp.where(z + 1 < nz, 1, 0) + jnp.where(z >= 1, 1, 0)
    pl.semaphore_wait(barrier, 3 + ends)

    y_states.start()
    own_states.start()
    wx[0].start()
    for m in range(3):
        wy[m].start()
    wx[1].start()
    own_states.wait()
    first(0)
    for m in range(3):
        loc[m].start()
    y_states.wait_recv()
    first(1)
    for s in range(nz - 1):
        relay(1, s)
        if s == 0:
            wy[0].wait_recv()
            wr[0].start()
    wy[1].wait_recv()
    wr[1].start()
    relay(0, 0)
    settle(1)
    norm(1)
    for s in range(1, nz - 1):
        if s == nz - 2:
            for m in range(2):
                loc[m].wait()
            block_product(b, 0)
            block_product(by, 1)
            for m in range(2):
                wx[m].wait_recv()
            block_product(bx, 2)
            wy[2].wait_recv()

            @pl.when(y == 0)
            def _():
                wx[2].start()
                wr[2].start()

            @pl.when(y == 1)
            def _():
                wr[2].start()
                wx[2].start()

        relay(0, s)
    settle(0)
    for j in range(4):
        R[:, pl.ds(j * w, w)] = X[
            pl.ds(pl.multiple_of(y * rows + z * own_rows, own_rows), own_rows),
            pl.ds(pl.multiple_of(blocks[j] * cols + k * w, w), w),
        ].astype(jnp.float32)
    norm(0)
    for m in range(2):
        wr[m].wait_recv()
    block_product(bd, 3)
    loc[2].wait()

    base = full // 2

    def down_cols(j, core):
        return pl.ds(pl.multiple_of(blocks[j] * cols + core * w, w), w)

    def block_rows(t):
        return pl.ds(pl.multiple_of((y if t == 0 else 1 - y) * rows, rows), rows)

    def sib_sum(t, j):
        return remote(
            X.at[block_rows(t), pl.ds(j * w, w)], SR.at[j, block_rows(t), :],
            c_sib.at[t, j], to_sib,
        )

    hw = w // 2

    def y_sum(j, h):
        return remote(
            X.at[block_rows(1), pl.ds(base + j * w + h * hw, hw)],
            YR.at[j, :, pl.ds(h * hw, hw)], c_y.at[j, h], to_y,
        )

    def z_sum(j, h, dz):
        to = lax.rem(z + dz, nz)
        return remote(
            X.at[
                pl.ds(pl.multiple_of(y * rows + to * own_rows, own_rows), own_rows),
                pl.ds(base + j * w + h * hw, hw),
            ],
            ZR.at[j, dz - 1, :, pl.ds(h * hw, hw)], c_z.at[j, h, dz - 1], at_z(to),
        )

    def strips(t):
        start = (y if t == 0 else 1 - y) * rows
        return lambda i: pl.ds(pl.multiple_of(start + i * strip, strip), strip)

    def step_a(t, j):
        @pl.loop(0, rows // strip)
        def _(i):
            r = strips(t)(i)
            X[r, pl.ds(j * w, w)] = jnp.dot(
                H[r, :], W[:, down_cols(j, 1 - k)], preferred_element_type=jnp.float32
            ).astype(jnp.bfloat16)

        sib_sum(t, j).start()

    def step_b(t, j):
        sib_sum(t, j).wait_recv()
        for h in range(2):
            down = pl.ds(pl.multiple_of(blocks[j] * cols + k * w + h * hw, hw), hw)

            @pl.loop(0, rows // strip)
            def _(i):
                r = strips(t)(i)
                X[r, pl.ds(base + j * w + h * hw, hw)] = (
                    jnp.dot(H[r, :], W[:, down], preferred_element_type=jnp.float32)
                    + SR[j, r, pl.ds(h * hw, hw)].astype(jnp.float32)
                ).astype(jnp.bfloat16)

            if t == 1:
                y_sum(j, h).start()

    def half_c(j, h):
        y_sum(j, h).wait_recv()

        @pl.loop(0, rows // own_rows)
        def _(i):
            r = pl.ds(pl.multiple_of(y * rows + i * own_rows, own_rows), own_rows)
            here = pl.ds(base + j * w + h * hw, hw)
            q = pl.ds(pl.multiple_of(i * own_rows, own_rows), own_rows)
            X[r, here] = (
                X[r, here].astype(jnp.float32)
                + YR[j, q, pl.ds(h * hw, hw)].astype(jnp.float32)
            ).astype(jnp.bfloat16)

        for dz in range(1, nz):
            z_sum(j, h, dz).start()

    def step_c(j):
        half_c(j, 0)
        half_c(j, 1)

    def half_e(j, h):
        here = pl.ds(j * w + h * hw, hw)
        total = R[:, here] + X[
            pl.ds(pl.multiple_of(y * rows + z * own_rows, own_rows), own_rows),
            pl.ds(base + j * w + h * hw, hw),
        ].astype(jnp.float32)
        for dz in range(1, nz):
            z_sum(j, h, dz).wait_recv()
            total = total + ZR[j, dz - 1, :, pl.ds(h * hw, hw)].astype(jnp.float32)
        R[:, here] = total

    def step_e(j):
        half_e(j, 0)
        half_e(j, 1)

    def down_from_x(low):
        @pl.when(y == (0 if low else 1))
        def _():
            wx[2].wait_recv()

        @pl.when(y == (1 if low else 0))
        def _():
            wr[2].wait_recv()

    bits = hash_ref.shape[1]
    side = bits // 2

    def fetch(q, j):
        return pltpu.make_async_copy(
            hash_ref.at[
                pl.ds(pl.multiple_of(blocks[j] * cols + k * w, w), w),
                pl.ds(q * side, side),
            ],
            G.at[pl.ds(q * base + j * w, w), pl.ds(0, side)],
            h_sem.at[q, j],
        )

    def swap(buf, sems):
        return remote(buf.at[0], buf.at[1], sems, to_sib)

    chips = lax.axis_size("batch") * nz
    me = b * nz + z
    docs = own_rows // DOC_LEN

    def tell(far):
        to = lax.rem(me + far, chips)
        return pltpu.make_async_remote_copy(
            src_ref=CA.at[me], dst_ref=CA.at[me],
            send_sem=a_send.at[far - 1], recv_sem=a_recv.at[far - 1],
            device_id={"batch": to // nz, "corpus": to % nz * 2 + k},
            device_id_type=pl.DeviceIdType.MESH,
        )

    def heard(far):
        src = lax.rem(me + chips - far, chips)
        return pltpu.make_async_remote_copy(
            src_ref=CA.at[src], dst_ref=CA.at[src],
            send_sem=a_send.at[far - 1], recv_sem=a_recv.at[far - 1],
            device_id={"batch": src // nz, "corpus": src % nz * 2 + k},
            device_id_type=pl.DeviceIdType.MESH,
        )

    def finish():
        square = jnp.sum(R[...] * R[...], axis=1, keepdims=True)
        SQ[0] = jnp.broadcast_to(square, SQ.shape[1:])
        swap(SQ, q_sem).start()
        swap(SQ, q_sem).wait()
        scale = lax.rsqrt((square + SQ[1][:, :1]) / float(full) + 1e-06)
        pooled = []
        for j in range(4):
            last = last_ref[:, pl.ds(pl.multiple_of(blocks[j] * cols + k * w, w), w)]
            final = R[:, pl.ds(j * w, w)] * scale * last
            pooled.append(
                jnp.concatenate(
                    [
                        jnp.mean(final[d * DOC_LEN : (d + 1) * DOC_LEN], axis=0, keepdims=True)
                        for d in range(docs)
                    ]
                    + [jnp.zeros((16 - docs, w), jnp.float32)],
                    axis=0,
                ).astype(jnp.bfloat16)
            )
        pooled = jnp.concatenate(pooled, axis=1)
        for q in range(2):
            for j in range(4):
                fetch(q, j).wait()
            PT[0, :, pl.ds(q * side, side)] = jnp.dot(
                pooled, G[pl.ds(q * base, base), pl.ds(0, side)],
                preferred_element_type=jnp.float32,
            )[: PT.shape[1]]
        swap(PT, p_sem).start()
        swap(PT, p_sem).wait()
        codes = jnp.tanh(PT[0] + PT[1])[:docs]
        lanes = CA.shape[2]
        CA[me] = jnp.concatenate(
            [codes[:, g * lanes : (g + 1) * lanes] for g in range(bits // lanes)], axis=0
        ).astype(jnp.bfloat16)

        @pl.loop(1, chips)
        def _(far):
            tell(far).start()

    tiles = rows // tile
    step_a(1, 0)
    step_a(1, 1)
    own_product(0, 1)
    step_b(1, 0)
    step_b(1, 1)
    own_product(1, tiles)
    wr[0].wait_send()
    wr[1].wait_send()
    for q in range(2):
        for j in range(4):
            fetch(q, j).start()
    step_a(0, 0)
    step_a(0, 1)
    down_from_x(True)
    step_a(1, 2)
    step_a(0, 2)
    step_b(0, 0)
    step_b(1, 2)
    step_c(0)
    step_b(0, 1)
    step_b(0, 2)
    step_c(1)
    down_from_x(False)
    step_a(1, 3)
    step_a(0, 3)
    step_b(1, 3)
    step_b(0, 3)
    step_e(0)
    step_c(2)
    half_c(3, 0)
    step_e(1)
    half_c(3, 1)
    step_e(2)
    step_e(3)
    finish()
    for j in range(4):
        sib_sum(0, j).wait_send()
        sib_sum(1, j).wait_send()
        for h in range(2):
            y_sum(j, h).wait_send()
            for dz in range(1, nz):
                z_sum(j, h, dz).wait_send()
    y_states.wait_send()
    for m in range(3):
        wx[m].wait_send()
        wy[m].wait_send()
    wr[2].wait_send()

    @pl.loop(1, chips)
    def _(far):
        heard(far).wait_recv()

    @pl.loop(1, chips)
    def _(far):
        tell(far).wait_send()

    out_ref[...] = CA[...]


def wide(states, norm_gain, gate_weight, up_weight, down_weight, final_gain, hash_weight):
    nz = lax.axis_size("corpus") // 2
    rows, feat = states.shape
    full = norm_gain.shape[0]
    half = gate_weight.shape[1] // 2
    cols = down_weight.shape[1]
    w = cols // 2
    own_rows = rows // nz
    bits = hash_weight.shape[1]
    chips = lax.axis_size("batch") * nz
    packed = own_rows // DOC_LEN * (bits // 128)
    dma = pltpu.SemaphoreType.DMA
    any_spec = pl.BlockSpec(memory_space=pl.ANY)
    vmem = pl.BlockSpec(memory_space=pltpu.VMEM)
    return pl.pallas_call(
        wide_kernel,
        out_shape=jax.ShapeDtypeStruct((chips, packed, 128), jnp.bfloat16),
        in_specs=[any_spec, vmem, any_spec, any_spec, any_spec, vmem, any_spec],
        out_specs=vmem,
        scratch_shapes=[
            pltpu.VMEM((2 * rows, full), jnp.bfloat16),
            pltpu.VMEM((full, half), jnp.bfloat16),
            pltpu.VMEM((full, half), jnp.bfloat16),
            pltpu.VMEM((half, full), jnp.bfloat16),
            pltpu.VMEM((rows, half), jnp.float32),
            pltpu.VMEM((rows, half), jnp.float32),
            pltpu.VMEM((2 * rows, half), jnp.bfloat16),
            pltpu.VMEM((4, 2 * rows, w), jnp.bfloat16),
            pltpu.VMEM((4, rows, w), jnp.bfloat16),
            pltpu.VMEM((4, nz - 1, own_rows, w), jnp.bfloat16),
            pltpu.VMEM((own_rows, full // 2), jnp.float32),
            pltpu.VMEM((2, own_rows, 128), jnp.float32),
            pltpu.VMEM((2, 8, bits), jnp.float32),
            pltpu.VMEM((chips, packed, 128), jnp.bfloat16),
            dma, dma((2,)), dma((2, nz - 1, 2)), dma((2, nz - 1, 2)), dma((2, nz, 2)),
            dma((3,)), dma((3, 2)), dma((3, 2)), dma((3, 2)),
            dma((2, 4, 2)), dma((4, 2, 2)), dma((4, 2, nz - 1, 2)),
            dma((2, 4)), dma((2,)), dma((2,)), dma((chips - 1,)), dma((chips - 1,)),
        ],
        compiler_params=pltpu.CompilerParams(
            collective_id=0, has_side_effects=True, vmem_limit_bytes=67043328
        ),
    )(
        states, norm_gain[None], gate_weight, up_weight, down_weight, final_gain[None],
        hash_weight,
    )


def plain_codes(
    states, norm_gain, gate_weight, up_weight, down_weight, final_gain, hash_weight
):
    whole = lax.all_gather(states, "corpus", axis=1, tiled=True)
    normed = rms(whole.astype(jnp.float32), norm_gain).astype(jnp.bfloat16)

    def add_one(piece):
        return add_rows(normed, piece)

    gate = add_one(lax.all_gather(gate_weight, "batch", axis=0, tiled=True))
    up = add_one(lax.all_gather(up_weight, "batch", axis=0, tiled=True))
    hidden = (jax.nn.silu(gate) * up).astype(jnp.bfloat16)
    terms = jnp.dot(
        hidden,
        lax.all_gather(down_weight, "batch", axis=1, tiled=True),
        preferred_element_type=jnp.float32,
    )
    ffn = lax.psum_scatter(
        terms.astype(jnp.bfloat16), "corpus", scatter_dimension=0, tiled=True
    ).astype(jnp.float32)
    own_rows = ffn.shape[0]
    mine = lax.dynamic_slice_in_dim(whole, lax.axis_index("corpus") * own_rows, own_rows, 0)
    resid = mine.astype(jnp.float32) + ffn
    finals = rms(resid, final_gain)
    owned_docs = own_rows // DOC_LEN
    pooled = jnp.mean(finals.reshape(owned_docs, DOC_LEN, finals.shape[1]), axis=1).astype(
        jnp.bfloat16
    )
    codes = jnp.tanh(jnp.dot(pooled, hash_weight, preferred_element_type=jnp.float32)).astype(
        jnp.bfloat16
    )
    return lax.all_gather(codes, ("batch", "corpus"), axis=0, tiled=True)


def local(
    states,
    norm_gain,
    gate_weight,
    up_weight,
    down_weight,
    final_gain,
    hash_weight,
    query_bits,
    slot_map,
    query_index,
):
    corpus_count = lax.axis_size("corpus")
    devices = lax.axis_size("batch") * corpus_count
    flat_index = lax.axis_index("batch") * corpus_count + lax.axis_index("corpus")
    layer = (states, norm_gain, gate_weight, up_weight, down_weight, final_gain, hash_weight)
    if lax.axis_size("batch") == 4 and corpus_count == 8:
        gathered = wide(*layer)
    else:
        gathered = plain_codes(*layer)
    query_rows = query_bits.shape[0] // devices
    return score(query_bits, gathered, slot_map, query_index, flat_index, query_rows)


def solution(mesh):
    placed = (
        P("batch", "corpus"),
        P(),
        P("batch", "corpus"),
        P("batch", "corpus"),
        P("corpus", "batch"),
        P(),
        P(),
        P(),
        P(),
        P(),
    )
    return jax.shard_map(
        local, mesh=mesh, in_specs=placed, out_specs=P(("batch", "corpus"), None), check_vma=False
    )
```

```python
import jax
import jax.numpy as jnp
from jax import lax
from jax.experimental import pallas as pl
from jax.experimental.pallas import tpu as pltpu
from jax.sharding import PartitionSpec as P

DOC_LEN = 64

EARLY = (0,)
DIRECT = (8,)

PLAN = (
    "a1 a2 a0 b1",
    "a3 b2 b0 b3",
    "own A0 A1 A2",
    "A3 B0 c0 B1",
    "B2 B3 c1 w4",
    "a4 A4 q0 b4",
    "B4 d0 c2 d1",
    "w5 a5 A5 b5",
    "B5 c3 d2 e0",
    "c4 d3 w6 a6",
    "A6 b6 B6 e1",
    "c5 d4 w7 a7",
    "A7 b7 B7 w8",
    "a8 A8 b8 B8",
    "e2 c6 d5 e3",
    "e4 c7 d6 c8",
    "d7 e5 e6 e7",
    "e8",
)


def pieces_of(w):
    full = [(j, h * w // 2, w // 2) for j in range(4) for h in range(2)]
    return full[:-1] + [(3, w // 2 + h * w // 4, w // 4) for h in range(2)]


def rms(values, gain):
    return values * lax.rsqrt(jnp.mean(values * values, axis=-1, keepdims=True) + 1e-06) * gain


def add_rows(left, piece):
    return jnp.dot(left, piece, preferred_element_type=jnp.float32)


def score_kernel(place_ref, bits_ref, codes_ref, slot_ref, index_ref, out_ref, picks):
    docs = slot_ref.shape[1]
    lanes = picks.shape[0]
    top = index_ref.shape[0]
    if len(codes_ref.shape) == 3:
        chips, packed, width = codes_ref.shape
        groups = bits_ref.shape[1] // width
        each = packed // groups
        every = codes_ref[...].astype(jnp.float32)
        codes = jnp.concatenate(
            [
                jnp.concatenate(
                    [every[n, g * each : (g + 1) * each] for n in range(chips)], axis=0
                )
                for g in range(groups)
            ],
            axis=1,
        ).astype(jnp.bfloat16)
    else:
        codes = codes_ref[...]
    entry = lax.broadcasted_iota(jnp.int32, (lanes, docs), 0)
    placing = jnp.where(entry == slot_ref[...], 1.0, 0.0).astype(jnp.bfloat16)
    corpus = jnp.dot(placing, codes, preferred_element_type=jnp.float32).astype(jnp.bfloat16)
    table = lax.dot_general(
        bits_ref[...],
        corpus,
        (((1,), (1,)), ((), ())),
        preferred_element_type=jnp.float32,
    ) * (1.0 / float(bits_ref.shape[1]) ** 0.5)
    picks[...] = jnp.zeros_like(picks)
    picks[:top, :] = index_ref[...]
    out_ref[...] = jnp.take_along_axis(table, picks[...].T, axis=1).T[:top, :]


def score(query_bits, codes, slot_map, query_index, flat_index, rows):
    docs = slot_map.shape[0]
    bits = query_bits.shape[1]
    top = query_index.shape[1]
    lanes = 128 * max(pl.cdiv(docs, 128), pl.cdiv(top, 128))
    index = query_index.T
    if rows % 128 == 0:
        index_spec = pl.BlockSpec((top, rows), lambda i, f: (0, f[0]))
    else:
        index = lax.dynamic_slice_in_dim(index, flat_index * rows, rows, 1)
        index_spec = pl.BlockSpec((top, rows), lambda i, f: (0, 0))
    out = pl.pallas_call(
        score_kernel,
        out_shape=jax.ShapeDtypeStruct((top, rows), jnp.float32),
        grid_spec=pltpu.PrefetchScalarGridSpec(
            num_scalar_prefetch=1,
            grid=(1,),
            in_specs=[
                pl.BlockSpec((rows, bits), lambda i, f: (f[0], 0)),
                pl.BlockSpec(codes.shape, lambda i, f: (0,) * codes.ndim),
                pl.BlockSpec((1, docs), lambda i, f: (0, 0)),
                index_spec,
            ],
            out_specs=pl.BlockSpec((top, rows), lambda i, f: (0, 0)),
            scratch_shapes=[pltpu.VMEM((lanes, rows), jnp.int32)],
        ),
    )(flat_index.reshape(1), query_bits, codes, slot_map[None], index)
    return out.T


def wide_kernel(
    states_ref, gain_ref, gate_ref, up_ref, down_ref, last_ref, hash_ref, out_ref,
    X, G, U, W, AG, AU, H, SR, YR, ZR, ZQ, R, SQ, PT, CA,
    s_loc, s_y, s_zr, s_zl, s_sib, w_loc, w_x, w_y, w_r, w_d, c_sib, c_y, c_z, c_q,
    h_sem, q_sem, p_sem, a_send, a_recv,
):
    nz = lax.axis_size("corpus") // 2
    b = lax.axis_index("batch")
    c = lax.axis_index("corpus")
    y, x = b // 2, b % 2
    z, k = c // 2, c % 2
    rows, feat = states_ref.shape
    half = W.shape[0]
    full = X.shape[1]
    cols = down_ref.shape[1]
    w = cols // 2
    by, bx, bd = (1 - y) * 2 + x, y * 2 + (1 - x), (1 - y) * 2 + (1 - x)
    to_y = {"batch": by}
    to_x = {"batch": bx}
    to_sib = {"corpus": z * 2 + (1 - k)}

    def at_z(other):
        return {"corpus": other * 2 + k}

    def remote(src, dst, sems, place):
        return pltpu.make_async_remote_copy(
            src_ref=src, dst_ref=dst, send_sem=sems.at[0], recv_sem=sems.at[1],
            device_id=place, device_id_type=pl.DeviceIdType.MESH,
        )

    def spot(t, zs, ks):
        block = y if t == 0 else 1 - y
        return X.at[
            pl.ds(pl.multiple_of(block * rows, rows), rows),
            pl.ds(pl.multiple_of((zs * 2 + ks) * feat, feat), feat),
        ]

    own_states = pltpu.make_async_copy(states_ref, spot(0, z, k), s_loc)
    y_states = remote(states_ref, X.at[
        pl.ds(pl.multiple_of(y * rows, rows), rows),
        pl.ds(pl.multiple_of(c * feat, feat), feat),
    ], s_y, to_y)

    def right(t, s):
        src = states_ref if t == 0 and s == 0 else spot(t, z - s, k)
        return remote(src, spot(t, z - s, k), s_zr.at[t, s], at_z(z + 1))

    def left(t, s):
        src = states_ref if t == 0 and s == 0 else spot(t, z + s, k)
        return remote(src, spot(t, z + s, k), s_zl.at[t, s], at_z(z - 1))

    def sib(t, zs):
        return remote(spot(t, zs, k), spot(t, zs, k), s_sib.at[t, zs], to_sib)

    def sib_in(t, zs):
        return remote(spot(t, zs, 1 - k), spot(t, zs, 1 - k), s_sib.at[t, zs], to_sib)

    def first(t):
        @pl.when(z + 1 < nz)
        def _():
            right(t, 0).start()

        @pl.when(z >= 1)
        def _():
            left(t, 0).start()

        sib(t, z).start()

    def relay(t, s):
        @pl.when(z - 1 - s >= 0)
        def _():
            right(t, s).wait_recv()
            if s + 1 < nz - 1:
                @pl.when(z + 1 < nz)
                def _():
                    right(t, s + 1).start()
            sib(t, z - 1 - s).start()

        @pl.when(z + 1 + s < nz)
        def _():
            left(t, s).wait_recv()
            if s + 1 < nz - 1:
                @pl.when(z >= 1)
                def _():
                    left(t, s + 1).start()
            sib(t, z + 1 + s).start()

    def part(m, mine):
        h = pl.ds(pl.multiple_of((y if mine else 1 - y) * half, half), half)
        if m == 2:
            return down_ref.at[h, :]
        return (gate_ref, up_ref)[m].at[:, h]

    def place(m, block):
        if m == 2:
            return W.at[:, pl.ds(pl.multiple_of(block * cols, cols), cols)]
        return (G, U)[m].at[pl.ds(pl.multiple_of(block * rows_w, rows_w), rows_w), :]

    rows_w = gate_ref.shape[0]
    loc = [pltpu.make_async_copy(part(m, True), place(m, b), w_loc.at[m]) for m in range(3)]
    wx = [remote(part(m, True), place(m, b), w_x.at[m], to_x) for m in range(2)]
    wy = [remote(part(m, False), place(m, b), w_y.at[m], to_y) for m in range(3)]
    wr = [remote(place(m, by), place(m, by), w_r.at[m], to_x) for m in range(2)]
    pieces = pieces_of(w)

    def down_pair(j, p):
        _, off, width = pieces[p]
        return W.at[
            :, pl.ds(pl.multiple_of(blocks[j] * cols + 2 * off, 2 * width), 2 * width)
        ]

    def down_x(p):
        src = down_pair(pieces[p][0] - 2, p)
        return remote(src, src, w_d.at[p], to_x)

    late = [p for p in range(len(pieces)) if pieces[p][0] >= 2]
    blocks = [x, 2 + x, 1 - x, 2 + (1 - x)]

    def settle(t):
        for zs in range(nz):
            sib_in(t, zs).wait_recv()
            sib(t, zs).wait_send()
        for s in range(nz - 1):
            @pl.when((z - s >= 0) & (z + 1 < nz))
            def _():
                right(t, s).wait_send()

            @pl.when((z + s < nz) & (z >= 1))
            def _():
                left(t, s).wait_send()

    gain = gain_ref[...]
    strip = min(512, rows)
    tile = min(256, rows)
    step = half // 3 if half % 384 == 0 else 128
    own_rows = R.shape[0]

    def block_rows(t):
        return pl.ds(pl.multiple_of((y if t == 0 else 1 - y) * rows, rows), rows)

    def own_unit(t, first, units=1):
        start = (y if t == 0 else 1 - y) * rows
        return pl.ds(pl.multiple_of(start + first * own_rows, own_rows), units * own_rows)

    def spots(p, shift=0):
        j, off, width = pieces[p]
        return pl.ds(shift + j * w + off, width)

    def here_cols(p, core):
        j, off, width = pieces[p]
        return pl.ds(pl.multiple_of(blocks[j] * cols + 2 * off + core * width, width), width)

    def norm(t):
        start = (y if t == 0 else 1 - y) * rows

        @pl.loop(0, rows // 32)
        def _(p):
            r = pl.ds(pl.multiple_of(start + p * 32, 32), 32)
            v = X[r, :].astype(jnp.float32)
            scale = lax.rsqrt(jnp.mean(v * v, axis=-1, keepdims=True) + 1e-06)
            X[r, :] = (v * scale * gain).astype(jnp.bfloat16)

    def block_product(block, order):
        depth = pl.ds(pl.multiple_of(block * rows_w, rows_w), rows_w)

        @pl.loop(0, rows // strip)
        def _(i):
            here = pl.ds(pl.multiple_of(i * strip, strip), strip)
            r = pl.ds(pl.multiple_of((1 - y) * rows + i * strip, strip), strip)

            @pl.loop(0, half // step)
            def _(j):
                h = pl.ds(pl.multiple_of(j * step, 128), step)
                g = jnp.dot(X[r, depth], G[depth, h], preferred_element_type=jnp.float32)
                u = jnp.dot(X[r, depth], U[depth, h], preferred_element_type=jnp.float32)
                if order > 0:
                    g = g + AG[here, h]
                    u = u + AU[here, h]
                if order < 3:
                    AG[here, h] = g
                    AU[here, h] = u
                else:
                    H[r, h] = (g * jax.nn.sigmoid(g) * u).astype(jnp.bfloat16)

    def own_product(low, high):
        @pl.loop(low, high)
        def _(i):
            r = pl.ds(pl.multiple_of(y * rows + i * tile, tile), tile)

            @pl.loop(0, half // step)
            def _(j):
                h = pl.ds(pl.multiple_of(j * step, 128), step)
                g = jnp.dot(X[r, :], G[:, h], preferred_element_type=jnp.float32)
                u = jnp.dot(X[r, :], U[:, h], preferred_element_type=jnp.float32)
                H[r, h] = (g * jax.nn.sigmoid(g) * u).astype(jnp.bfloat16)

    barrier = pltpu.get_barrier_semaphore()

    def greet(place):
        pl.semaphore_signal(
            barrier, inc=1, device_id=place, device_id_type=pl.DeviceIdType.MESH
        )

    greet(to_y)
    greet(to_x)
    greet(to_sib)

    @pl.when(z + 1 < nz)
    def _():
        greet(at_z(z + 1))

    @pl.when(z >= 1)
    def _():
        greet(at_z(z - 1))

    ends = jnp.where(z + 1 < nz, 1, 0) + jnp.where(z >= 1, 1, 0)
    pl.semaphore_wait(barrier, 3 + ends)

    y_states.start()
    own_states.start()
    wx[0].start()
    for m in range(3):
        wy[m].start()
    wx[1].start()
    own_states.wait()
    first(0)
    for m in range(3):
        loc[m].start()
    y_states.wait_recv()
    first(1)
    for s in range(nz - 1):
        relay(1, s)
        if s == 0:
            wy[0].wait_recv()
            wr[0].start()
    wy[1].wait_recv()
    wr[1].start()
    relay(0, 0)
    settle(1)
    norm(1)
    for s in range(1, nz - 1):
        if s == nz - 2:
            for m in range(2):
                loc[m].wait()
            block_product(b, 0)
            block_product(by, 1)
            for m in range(2):
                wx[m].wait_recv()
            block_product(bx, 2)
            loc[2].wait()
            wy[2].wait_recv()
            for p in late:
                down_x(p).start()

        relay(0, s)
    settle(0)
    for p in range(len(pieces)):
        R[:, spots(p)] = X[own_unit(0, z), here_cols(p, k)].astype(jnp.float32)
    norm(0)
    for m in range(2):
        wr[m].wait_recv()
    block_product(bd, 3)

    base = full // 2
    inner = (z == 1) | (z == 2)
    outer = (z == 0) | (z == 3)

    def sib_sum(t, p):
        return remote(
            X.at[block_rows(t), spots(p)], SR.at[block_rows(t), spots(p)], c_sib.at[t, p], to_sib
        )

    def y_sum(p):
        return remote(X.at[block_rows(1), spots(p, base)], YR.at[:, spots(p)], c_y.at[p], to_y)

    def y_early(p):
        return remote(
            X.at[own_unit(1, z), spots(p, base)], YR.at[pl.ds(0, own_rows), spots(p)],
            c_y.at[p], to_y,
        )

    def z_early(p, dz):
        to = lax.rem(z + dz, nz)
        return remote(
            X.at[own_unit(1, to), spots(p, base)], ZQ.at[dz - 1, :, spots(p)],
            c_q.at[p, dz - 1], at_z(to),
        )

    def z_sum(p, dz):
        to = lax.rem(z + dz, nz)
        return remote(
            X.at[own_unit(0, to), spots(p, base)],
            ZR.at[pl.ds((dz - 1) * own_rows, own_rows), spots(p)], c_z.at[p, dz - 1], at_z(to),
        )

    def z_in(p):
        first = jnp.where(z == 0, 1, 0)
        return remote(
            X.at[own_unit(0, first, 3), spots(p, base)],
            ZR.at[pl.ds(0, 3 * own_rows), spots(p)], c_z.at[p, 0],
            at_z(jnp.where(z == 0, 1, 2)),
        )

    def z_out(p):
        to = jnp.where(z == 1, 0, 3)
        return remote(
            X.at[own_unit(0, to), spots(p, base)],
            ZR.at[pl.ds(0, own_rows), spots(p)], c_z.at[p, 1], at_z(to),
        )

    def z_far(p, step):
        to = jnp.where(z == 1, 2, 1) if step == 1 else jnp.where(z == 1, 3, 0)
        return remote(
            X.at[own_unit(0, to), spots(p, base)],
            ZR.at[pl.ds(3 * own_rows, own_rows), spots(p)], c_z.at[p, 1 + step], at_z(to),
        )

    def strips(t):
        start = (y if t == 0 else 1 - y) * rows
        return lambda i: pl.ds(pl.multiple_of(start + i * strip, strip), strip)

    def step_a(t, p):
        @pl.loop(0, rows // strip)
        def _(i):
            r = strips(t)(i)
            X[r, spots(p)] = jnp.dot(
                H[r, :], W[:, here_cols(p, 1 - k)], preferred_element_type=jnp.float32
            ).astype(jnp.bfloat16)

        sib_sum(t, p).start()

    def step_b(t, p):
        sib_sum(t, p).wait_recv()

        @pl.loop(0, rows // strip)
        def _(i):
            r = strips(t)(i)
            X[r, spots(p, base)] = (
                jnp.dot(H[r, :], W[:, here_cols(p, k)], preferred_element_type=jnp.float32)
                + SR[r, spots(p)].astype(jnp.float32)
            ).astype(jnp.bfloat16)

        if t == 1 and p in EARLY:
            for dz in (2, 3, 1):
                z_early(p, dz).start()
        elif t == 1:
            y_sum(p).start()

    def step_q(p):
        total = X[own_unit(1, z), spots(p, base)].astype(jnp.float32)
        for dz in range(1, nz):
            z_early(p, dz).wait_recv()
            total = total + ZQ[dz - 1, :, spots(p)].astype(jnp.float32)
        X[own_unit(1, z), spots(p, base)] = total.astype(jnp.bfloat16)
        y_early(p).start()

    def step_c(p):
        if p not in EARLY:
            y_sum(p).wait_recv()

            @pl.loop(0, rows // own_rows)
            def _(i):
                r = own_unit(0, i)
                q = pl.ds(pl.multiple_of(i * own_rows, own_rows), own_rows)
                X[r, spots(p, base)] = (
                    X[r, spots(p, base)].astype(jnp.float32) + YR[q, spots(p)].astype(jnp.float32)
                ).astype(jnp.bfloat16)

        if p in DIRECT:
            for dz in (2, 3, 1):
                z_sum(p, dz).start()
        else:
            @pl.when(outer)
            def _():
                z_in(p).start()

            @pl.when(inner)
            def _():
                z_out(p).start()

    def step_d(p):
        if p not in DIRECT:
            @pl.when(inner)
            def _():
                z_in(p).wait_recv()
                r = own_unit(0, jnp.where(z == 1, 2, 0), 2)
                q = pl.ds(pl.multiple_of(jnp.where(z == 1, own_rows, 0), own_rows), 2 * own_rows)
                X[r, spots(p, base)] = (
                    X[r, spots(p, base)].astype(jnp.float32) + ZR[q, spots(p)].astype(jnp.float32)
                ).astype(jnp.bfloat16)
                z_far(p, 2).start()
                z_far(p, 1).start()

    def step_e(p):
        total = R[:, spots(p)] + X[own_unit(0, z), spots(p, base)].astype(jnp.float32)
        if p in EARLY:
            y_early(p).wait_recv()
            total = total + YR[pl.ds(0, own_rows), spots(p)].astype(jnp.float32)
        if p in DIRECT:
            for dz in range(1, nz):
                z_sum(p, dz).wait_recv()
                total = total + ZR[pl.ds((dz - 1) * own_rows, own_rows), spots(p)].astype(
                    jnp.float32
                )
        else:
            @pl.when(outer)
            def _():
                z_out(p).wait_recv()
                z_far(p, 2).wait_recv()

            @pl.when(inner)
            def _():
                z_far(p, 1).wait_recv()

            q = pl.ds(
                pl.multiple_of(jnp.where(z == 2, 2 * own_rows, 0), own_rows), own_rows
            )
            total = total + ZR[q, spots(p)].astype(jnp.float32)
            total = total + ZR[pl.ds(3 * own_rows, own_rows), spots(p)].astype(jnp.float32)
        R[:, spots(p)] = total

    bits = hash_ref.shape[1]
    side = bits // 2

    def fetch(q, p):
        return pltpu.make_async_copy(
            hash_ref.at[here_cols(p, k), pl.ds(q * side, side)],
            G.at[spots(p, q * base), pl.ds(0, side)],
            h_sem.at[q, p],
        )

    def swap(buf, sems):
        return remote(buf.at[0], buf.at[1], sems, to_sib)

    chips = lax.axis_size("batch") * nz
    me = b * nz + z
    docs = own_rows // DOC_LEN

    def tell(far):
        to = lax.rem(me + far, chips)
        return pltpu.make_async_remote_copy(
            src_ref=CA.at[me], dst_ref=CA.at[me],
            send_sem=a_send.at[far - 1], recv_sem=a_recv.at[far - 1],
            device_id={"batch": to // nz, "corpus": to % nz * 2 + k},
            device_id_type=pl.DeviceIdType.MESH,
        )

    def heard(far):
        src = lax.rem(me + chips - far, chips)
        return pltpu.make_async_remote_copy(
            src_ref=CA.at[src], dst_ref=CA.at[src],
            send_sem=a_send.at[far - 1], recv_sem=a_recv.at[far - 1],
            device_id={"batch": src // nz, "corpus": src % nz * 2 + k},
            device_id_type=pl.DeviceIdType.MESH,
        )

    def finish():
        square = jnp.sum(R[...] * R[...], axis=1, keepdims=True)
        SQ[0] = jnp.broadcast_to(square, SQ.shape[1:])
        swap(SQ, q_sem).start()
        swap(SQ, q_sem).wait()
        scale = lax.rsqrt((square + SQ[1][:, :1]) / float(full) + 1e-06)
        pooled = []
        for p in range(len(pieces)):
            final = R[:, spots(p)] * scale * last_ref[:, here_cols(p, k)]
            pooled.append(
                jnp.concatenate(
                    [
                        jnp.mean(final[d * DOC_LEN : (d + 1) * DOC_LEN], axis=0, keepdims=True)
                        for d in range(docs)
                    ]
                    + [jnp.zeros((16 - docs, pieces[p][2]), jnp.float32)],
                    axis=0,
                ).astype(jnp.bfloat16)
            )
        pooled = jnp.concatenate(pooled, axis=1)
        for q in range(2):
            for p in range(len(pieces)):
                fetch(q, p).wait()
            PT[0, :, pl.ds(q * side, side)] = jnp.dot(
                pooled, G[pl.ds(q * base, base), pl.ds(0, side)],
                preferred_element_type=jnp.float32,
            )[: PT.shape[1]]
        swap(PT, p_sem).start()
        swap(PT, p_sem).wait()
        codes = jnp.tanh(PT[0] + PT[1])[:docs]
        lanes = CA.shape[2]
        CA[me] = jnp.concatenate(
            [codes[:, g * lanes : (g + 1) * lanes] for g in range(bits // lanes)], axis=0
        ).astype(jnp.bfloat16)

        @pl.loop(1, chips)
        def _(far):
            tell(far).start()

    tiles = rows // tile
    for act in [act for line in PLAN for act in line.split()]:
        if act == "own":
            own_product(0, tiles)
            wr[0].wait_send()
            wr[1].wait_send()
            for q in range(2):
                for p in range(len(pieces)):
                    fetch(q, p).start()
            continue
        kind, p = act[0], int(act[1:])
        if kind == "w":
            down_x(p).wait_recv()
        elif kind == "a":
            step_a(1, p)
        elif kind == "A":
            step_a(0, p)
        elif kind == "b":
            step_b(1, p)
        elif kind == "B":
            step_b(0, p)
        elif kind == "q":
            step_q(p)
        elif kind == "c":
            step_c(p)
        elif kind == "d":
            step_d(p)
        else:
            step_e(p)
    finish()
    for p in range(len(pieces)):
        sib_sum(0, p).wait_send()
        sib_sum(1, p).wait_send()
        if p in EARLY:
            y_early(p).wait_send()
            for dz in range(1, nz):
                z_early(p, dz).wait_send()
        else:
            y_sum(p).wait_send()
        if p in DIRECT:
            for dz in range(1, nz):
                z_sum(p, dz).wait_send()
            continue

        @pl.when(outer)
        def _(p=p):
            z_in(p).wait_send()

        @pl.when(inner)
        def _(p=p):
            z_out(p).wait_send()
            z_far(p, 1).wait_send()
            z_far(p, 2).wait_send()

    y_states.wait_send()
    for p in late:
        down_x(p).wait_send()
    for m in range(2):
        wx[m].wait_send()
    for m in range(3):
        wy[m].wait_send()

    @pl.loop(1, chips)
    def _(far):
        heard(far).wait_recv()

    @pl.loop(1, chips)
    def _(far):
        tell(far).wait_send()

    out_ref[...] = CA[...]


def wide(states, norm_gain, gate_weight, up_weight, down_weight, final_gain, hash_weight):
    nz = lax.axis_size("corpus") // 2
    rows, feat = states.shape
    full = norm_gain.shape[0]
    half = gate_weight.shape[1] // 2
    cols = down_weight.shape[1]
    w = cols // 2
    own_rows = rows // nz
    bits = hash_weight.shape[1]
    chips = lax.axis_size("batch") * nz
    packed = own_rows // DOC_LEN * (bits // 128)
    pieces = pieces_of(w)
    count = len(pieces)
    early = sum(pieces[p][2] for p in EARLY)
    dma = pltpu.SemaphoreType.DMA
    any_spec = pl.BlockSpec(memory_space=pl.ANY)
    vmem = pl.BlockSpec(memory_space=pltpu.VMEM)
    return pl.pallas_call(
        wide_kernel,
        out_shape=jax.ShapeDtypeStruct((chips, packed, 128), jnp.bfloat16),
        in_specs=[any_spec, vmem, any_spec, any_spec, any_spec, vmem, any_spec],
        out_specs=vmem,
        scratch_shapes=[
            pltpu.VMEM((2 * rows, full), jnp.bfloat16),
            pltpu.VMEM((full, half), jnp.bfloat16),
            pltpu.VMEM((full, half), jnp.bfloat16),
            pltpu.VMEM((half, full), jnp.bfloat16),
            pltpu.VMEM((rows, half), jnp.float32),
            pltpu.VMEM((rows, half), jnp.float32),
            pltpu.VMEM((2 * rows, half), jnp.bfloat16),
            pltpu.VMEM((2 * rows, full // 2), jnp.bfloat16),
            pltpu.VMEM((rows, full // 2), jnp.bfloat16),
            pltpu.VMEM((rows, full // 2), jnp.bfloat16),
            pltpu.VMEM((nz - 1, own_rows, early), jnp.bfloat16),
            pltpu.VMEM((own_rows, full // 2), jnp.float32),
            pltpu.VMEM((2, own_rows, 128), jnp.float32),
            pltpu.VMEM((2, 8, bits), jnp.float32),
            pltpu.VMEM((chips, packed, 128), jnp.bfloat16),
            dma, dma((2,)), dma((2, nz - 1, 2)), dma((2, nz - 1, 2)), dma((2, nz, 2)),
            dma((3,)), dma((2, 2)), dma((3, 2)), dma((2, 2)), dma((count, 2)),
            dma((2, count, 2)), dma((count, 2)), dma((count, 4, 2)),
            dma((len(EARLY), nz - 1, 2)), dma((2, count)), dma((2,)), dma((2,)), dma((chips - 1,)), dma((chips - 1,)),
        ],
        compiler_params=pltpu.CompilerParams(
            collective_id=0, has_side_effects=True, vmem_limit_bytes=67043328
        ),
    )(
        states, norm_gain[None], gate_weight, up_weight, down_weight, final_gain[None],
        hash_weight,
    )


def plain_codes(
    states, norm_gain, gate_weight, up_weight, down_weight, final_gain, hash_weight
):
    whole = lax.all_gather(states, "corpus", axis=1, tiled=True)
    normed = rms(whole.astype(jnp.float32), norm_gain).astype(jnp.bfloat16)

    def add_one(piece):
        return add_rows(normed, piece)

    gate = add_one(lax.all_gather(gate_weight, "batch", axis=0, tiled=True))
    up = add_one(lax.all_gather(up_weight, "batch", axis=0, tiled=True))
    hidden = (jax.nn.silu(gate) * up).astype(jnp.bfloat16)
    terms = jnp.dot(
        hidden,
        lax.all_gather(down_weight, "batch", axis=1, tiled=True),
        preferred_element_type=jnp.float32,
    )
    ffn = lax.psum_scatter(
        terms.astype(jnp.bfloat16), "corpus", scatter_dimension=0, tiled=True
    ).astype(jnp.float32)
    own_rows = ffn.shape[0]
    mine = lax.dynamic_slice_in_dim(whole, lax.axis_index("corpus") * own_rows, own_rows, 0)
    resid = mine.astype(jnp.float32) + ffn
    finals = rms(resid, final_gain)
    owned_docs = own_rows // DOC_LEN
    pooled = jnp.mean(finals.reshape(owned_docs, DOC_LEN, finals.shape[1]), axis=1).astype(
        jnp.bfloat16
    )
    codes = jnp.tanh(jnp.dot(pooled, hash_weight, preferred_element_type=jnp.float32)).astype(
        jnp.bfloat16
    )
    return lax.all_gather(codes, ("batch", "corpus"), axis=0, tiled=True)


def local(
    states,
    norm_gain,
    gate_weight,
    up_weight,
    down_weight,
    final_gain,
    hash_weight,
    query_bits,
    slot_map,
    query_index,
):
    corpus_count = lax.axis_size("corpus")
    devices = lax.axis_size("batch") * corpus_count
    flat_index = lax.axis_index("batch") * corpus_count + lax.axis_index("corpus")
    layer = (states, norm_gain, gate_weight, up_weight, down_weight, final_gain, hash_weight)
    if lax.axis_size("batch") == 4 and corpus_count == 8:
        gathered = wide(*layer)
    else:
        gathered = plain_codes(*layer)
    query_rows = query_bits.shape[0] // devices
    return score(query_bits, gathered, slot_map, query_index, flat_index, query_rows)


def solution(mesh):
    placed = (
        P("batch", "corpus"),
        P(),
        P("batch", "corpus"),
        P("batch", "corpus"),
        P("corpus", "batch"),
        P(),
        P(),
        P(),
        P(),
        P(),
    )
    return jax.shard_map(
        local, mesh=mesh, in_specs=placed, out_specs=P(("batch", "corpus"), None), check_vma=False
    )
```

```python
import jax
import jax.numpy as jnp
from jax import lax
from jax.experimental import pallas as pl
from jax.experimental.pallas import tpu as pltpu
from jax.sharding import PartitionSpec as P

DOC_LEN = 64

EARLY = (0,)
DIRECT = (8,)

PLAN = (
    "t a1 a2 a0",
    "b1 a3 b2 b0",
    "b3 r o0 o1",
    "hash A0 A1 B0",
    "c0 A2 B1 c1",
    "A3 B2 B3 w4",
    "a4 A4 q0 b4",
    "B4 d0 c2 d1",
    "w5 a5 A5 b5",
    "B5 c3 d2 e0",
    "c4 d3 w6 a6",
    "A6 b6 B6 e1",
    "c5 d4 w7 a7",
    "A7 b7 B7 w8",
    "a8 A8 b8 B8",
    "e2 c6 d5 e3",
    "e4 c7 d6 c8",
    "d7 e5 e6 e7",
    "e8",
)


def pieces_of(w):
    full = [(j, h * w // 2, w // 2) for j in range(4) for h in range(2)]
    return full[:-1] + [(3, w // 2 + h * w // 4, w // 4) for h in range(2)]


def rms(values, gain):
    return values * lax.rsqrt(jnp.mean(values * values, axis=-1, keepdims=True) + 1e-06) * gain


def add_rows(left, piece):
    return jnp.dot(left, piece, preferred_element_type=jnp.float32)


def score_kernel(place_ref, bits_ref, codes_ref, slot_ref, index_ref, out_ref, picks):
    docs = slot_ref.shape[1]
    lanes = picks.shape[0]
    top = index_ref.shape[0]
    if len(codes_ref.shape) == 3:
        chips, packed, width = codes_ref.shape
        groups = bits_ref.shape[1] // width
        each = packed // groups
        every = codes_ref[...].astype(jnp.float32)
        codes = jnp.concatenate(
            [
                jnp.concatenate(
                    [every[n, g * each : (g + 1) * each] for n in range(chips)], axis=0
                )
                for g in range(groups)
            ],
            axis=1,
        ).astype(jnp.bfloat16)
    else:
        codes = codes_ref[...]
    entry = lax.broadcasted_iota(jnp.int32, (lanes, docs), 0)
    placing = jnp.where(entry == slot_ref[...], 1.0, 0.0).astype(jnp.bfloat16)
    corpus = jnp.dot(placing, codes, preferred_element_type=jnp.float32).astype(jnp.bfloat16)
    table = lax.dot_general(
        bits_ref[...],
        corpus,
        (((1,), (1,)), ((), ())),
        preferred_element_type=jnp.float32,
    ) * (1.0 / float(bits_ref.shape[1]) ** 0.5)
    picks[...] = jnp.zeros_like(picks)
    picks[:top, :] = index_ref[...]
    out_ref[...] = jnp.take_along_axis(table, picks[...].T, axis=1).T[:top, :]


def score(query_bits, codes, slot_map, query_index, flat_index, rows):
    docs = slot_map.shape[0]
    bits = query_bits.shape[1]
    top = query_index.shape[1]
    lanes = 128 * max(pl.cdiv(docs, 128), pl.cdiv(top, 128))
    index = query_index.T
    if rows % 128 == 0:
        index_spec = pl.BlockSpec((top, rows), lambda i, f: (0, f[0]))
    else:
        index = lax.dynamic_slice_in_dim(index, flat_index * rows, rows, 1)
        index_spec = pl.BlockSpec((top, rows), lambda i, f: (0, 0))
    out = pl.pallas_call(
        score_kernel,
        out_shape=jax.ShapeDtypeStruct((top, rows), jnp.float32),
        grid_spec=pltpu.PrefetchScalarGridSpec(
            num_scalar_prefetch=1,
            grid=(1,),
            in_specs=[
                pl.BlockSpec((rows, bits), lambda i, f: (f[0], 0)),
                pl.BlockSpec(codes.shape, lambda i, f: (0,) * codes.ndim),
                pl.BlockSpec((1, docs), lambda i, f: (0, 0)),
                index_spec,
            ],
            out_specs=pl.BlockSpec((top, rows), lambda i, f: (0, 0)),
            scratch_shapes=[pltpu.VMEM((lanes, rows), jnp.int32)],
        ),
    )(flat_index.reshape(1), query_bits, codes, slot_map[None], index)
    return out.T


def wide_kernel(
    states_ref, gain_ref, gate_ref, up_ref, down_ref, last_ref, hash_ref, out_ref,
    X, G, U, W, AG, AU, H, SR, YR, ZR, ZQ, R, SQ, PT, CA,
    s_loc, s_y, s_zr, s_zl, s_sib, w_loc, w_x, w_y, w_r, w_d, c_sib, c_y, c_z, c_q,
    h_sem, q_sem, p_sem, a_send, a_recv,
):
    nz = lax.axis_size("corpus") // 2
    b = lax.axis_index("batch")
    c = lax.axis_index("corpus")
    y, x = b // 2, b % 2
    z, k = c // 2, c % 2
    rows, feat = states_ref.shape
    half = W.shape[0]
    full = X.shape[1]
    cols = down_ref.shape[1]
    w = cols // 2
    by, bx, bd = (1 - y) * 2 + x, y * 2 + (1 - x), (1 - y) * 2 + (1 - x)
    to_y = {"batch": by}
    to_x = {"batch": bx}
    to_sib = {"corpus": z * 2 + (1 - k)}

    def at_z(other):
        return {"corpus": other * 2 + k}

    def remote(src, dst, sems, place):
        return pltpu.make_async_remote_copy(
            src_ref=src, dst_ref=dst, send_sem=sems.at[0], recv_sem=sems.at[1],
            device_id=place, device_id_type=pl.DeviceIdType.MESH,
        )

    def spot(t, zs, ks):
        block = y if t == 0 else 1 - y
        return X.at[
            pl.ds(pl.multiple_of(block * rows, rows), rows),
            pl.ds(pl.multiple_of((zs * 2 + ks) * feat, feat), feat),
        ]

    own_states = pltpu.make_async_copy(states_ref, spot(0, z, k), s_loc)
    y_states = remote(states_ref, X.at[
        pl.ds(pl.multiple_of(y * rows, rows), rows),
        pl.ds(pl.multiple_of(c * feat, feat), feat),
    ], s_y, to_y)

    def right(t, s):
        src = states_ref if t == 0 and s == 0 else spot(t, z - s, k)
        return remote(src, spot(t, z - s, k), s_zr.at[t, s], at_z(z + 1))

    def left(t, s):
        src = states_ref if t == 0 and s == 0 else spot(t, z + s, k)
        return remote(src, spot(t, z + s, k), s_zl.at[t, s], at_z(z - 1))

    def sib(t, zs):
        return remote(spot(t, zs, k), spot(t, zs, k), s_sib.at[t, zs], to_sib)

    def sib_in(t, zs):
        return remote(spot(t, zs, 1 - k), spot(t, zs, 1 - k), s_sib.at[t, zs], to_sib)

    def first(t):
        @pl.when(z + 1 < nz)
        def _():
            right(t, 0).start()

        @pl.when(z >= 1)
        def _():
            left(t, 0).start()

        sib(t, z).start()

    def relay(t, s):
        @pl.when(z - 1 - s >= 0)
        def _():
            right(t, s).wait_recv()
            if s + 1 < nz - 1:
                @pl.when(z + 1 < nz)
                def _():
                    right(t, s + 1).start()
            sib(t, z - 1 - s).start()

        @pl.when(z + 1 + s < nz)
        def _():
            left(t, s).wait_recv()
            if s + 1 < nz - 1:
                @pl.when(z >= 1)
                def _():
                    left(t, s + 1).start()
            sib(t, z + 1 + s).start()

    def part(m, mine):
        h = pl.ds(pl.multiple_of((y if mine else 1 - y) * half, half), half)
        if m == 2:
            return down_ref.at[h, :]
        return (gate_ref, up_ref)[m].at[:, h]

    def place(m, block):
        if m == 2:
            return W.at[:, pl.ds(pl.multiple_of(block * cols, cols), cols)]
        return (G, U)[m].at[pl.ds(pl.multiple_of(block * rows_w, rows_w), rows_w), :]

    rows_w = gate_ref.shape[0]
    loc = [pltpu.make_async_copy(part(m, True), place(m, b), w_loc.at[m]) for m in range(3)]
    wx = [remote(part(m, True), place(m, b), w_x.at[m], to_x) for m in range(2)]
    wy = [remote(part(m, False), place(m, b), w_y.at[m], to_y) for m in range(3)]
    wr = [remote(place(m, by), place(m, by), w_r.at[m], to_x) for m in range(2)]
    pieces = pieces_of(w)

    def down_pair(j, p):
        _, off, width = pieces[p]
        return W.at[
            :, pl.ds(pl.multiple_of(blocks[j] * cols + 2 * off, 2 * width), 2 * width)
        ]

    def down_x(p):
        src = down_pair(pieces[p][0] - 2, p)
        return remote(src, src, w_d.at[p], to_x)

    late = [p for p in range(len(pieces)) if pieces[p][0] >= 2]
    blocks = [x, 2 + x, 1 - x, 2 + (1 - x)]

    def settle(t):
        for zs in range(nz):
            sib_in(t, zs).wait_recv()
            sib(t, zs).wait_send()
        for s in range(nz - 1):
            @pl.when((z - s >= 0) & (z + 1 < nz))
            def _():
                right(t, s).wait_send()

            @pl.when((z + s < nz) & (z >= 1))
            def _():
                left(t, s).wait_send()

    gain = gain_ref[...]
    strip = min(512, rows)
    tile = min(512, rows)
    step = half // 3 if half % 384 == 0 else 128
    own_rows = R.shape[0]

    def block_rows(t):
        return pl.ds(pl.multiple_of((y if t == 0 else 1 - y) * rows, rows), rows)

    def own_unit(t, first, units=1):
        start = (y if t == 0 else 1 - y) * rows
        return pl.ds(pl.multiple_of(start + first * own_rows, own_rows), units * own_rows)

    def spots(p, shift=0):
        j, off, width = pieces[p]
        return pl.ds(shift + j * w + off, width)

    def here_cols(p, core):
        j, off, width = pieces[p]
        return pl.ds(pl.multiple_of(blocks[j] * cols + 2 * off + core * width, width), width)

    def norm(t):
        start = (y if t == 0 else 1 - y) * rows

        @pl.loop(0, rows // 32)
        def _(p):
            r = pl.ds(pl.multiple_of(start + p * 32, 32), 32)
            v = X[r, :].astype(jnp.float32)
            scale = lax.rsqrt(jnp.mean(v * v, axis=-1, keepdims=True) + 1e-06)
            X[r, :] = (v * scale * gain).astype(jnp.bfloat16)

    def block_product(block, order):
        depth = pl.ds(pl.multiple_of(block * rows_w, rows_w), rows_w)

        @pl.loop(0, rows // strip)
        def _(i):
            here = pl.ds(pl.multiple_of(i * strip, strip), strip)
            r = pl.ds(pl.multiple_of((1 - y) * rows + i * strip, strip), strip)

            @pl.loop(0, half // step)
            def _(j):
                h = pl.ds(pl.multiple_of(j * step, 128), step)
                g = jnp.dot(X[r, depth], G[depth, h], preferred_element_type=jnp.float32)
                u = jnp.dot(X[r, depth], U[depth, h], preferred_element_type=jnp.float32)
                if order > 0:
                    g = g + AG[here, h]
                    u = u + AU[here, h]
                AG[here, h] = g
                AU[here, h] = u

    def last_gate():
        depth = pl.ds(pl.multiple_of(bd * rows_w, rows_w), rows_w)

        @pl.loop(0, rows // strip)
        def _(i):
            here = pl.ds(pl.multiple_of(i * strip, strip), strip)
            r = pl.ds(pl.multiple_of((1 - y) * rows + i * strip, strip), strip)

            @pl.loop(0, half // step)
            def _(j):
                h = pl.ds(pl.multiple_of(j * step, 128), step)
                g = AG[here, h] + jnp.dot(
                    X[r, depth], G[depth, h], preferred_element_type=jnp.float32
                )
                AG[here, h] = g * jax.nn.sigmoid(g)

    def last_up():
        depth = pl.ds(pl.multiple_of(bd * rows_w, rows_w), rows_w)

        @pl.loop(0, rows // strip)
        def _(i):
            here = pl.ds(pl.multiple_of(i * strip, strip), strip)
            r = pl.ds(pl.multiple_of((1 - y) * rows + i * strip, strip), strip)

            @pl.loop(0, half // step)
            def _(j):
                h = pl.ds(pl.multiple_of(j * step, 128), step)
                u = AU[here, h] + jnp.dot(
                    X[r, depth], U[depth, h], preferred_element_type=jnp.float32
                )
                H[r, h] = (AG[here, h] * u).astype(jnp.bfloat16)

    def rest():
        settle(0)
        for p in range(len(pieces)):
            R[:, spots(p)] = X[own_unit(0, z), here_cols(p, k)].astype(jnp.float32)
        norm(0)

    def own_product(low, high):
        @pl.loop(low, high)
        def _(i):
            r = pl.ds(pl.multiple_of(y * rows + i * tile, tile), tile)

            @pl.loop(0, half // step)
            def _(j):
                h = pl.ds(pl.multiple_of(j * step, 128), step)
                g = jnp.dot(X[r, :], G[:, h], preferred_element_type=jnp.float32)
                u = jnp.dot(X[r, :], U[:, h], preferred_element_type=jnp.float32)
                H[r, h] = (g * jax.nn.sigmoid(g) * u).astype(jnp.bfloat16)

    barrier = pltpu.get_barrier_semaphore()

    def greet(place):
        pl.semaphore_signal(
            barrier, inc=1, device_id=place, device_id_type=pl.DeviceIdType.MESH
        )

    greet(to_y)
    greet(to_x)
    greet(to_sib)

    @pl.when(z + 1 < nz)
    def _():
        greet(at_z(z + 1))

    @pl.when(z >= 1)
    def _():
        greet(at_z(z - 1))

    ends = jnp.where(z + 1 < nz, 1, 0) + jnp.where(z >= 1, 1, 0)
    pl.semaphore_wait(barrier, 3 + ends)

    y_states.start()
    own_states.start()
    wx[0].start()
    for m in range(3):
        wy[m].start()
    wx[1].start()
    own_states.wait()
    first(0)
    for m in range(3):
        loc[m].start()
    y_states.wait_recv()
    first(1)
    for s in range(nz - 1):
        relay(1, s)
        if s == 0:
            wy[0].wait_recv()
            wr[0].start()
    wy[1].wait_recv()
    wr[1].start()
    relay(0, 0)
    settle(1)
    norm(1)
    for s in range(1, nz - 2):
        relay(0, s)
    for m in range(2):
        loc[m].wait()
    block_product(b, 0)
    block_product(by, 1)
    for m in range(2):
        wx[m].wait_recv()
    block_product(bx, 2)
    wr[0].wait_recv()
    last_gate()
    loc[2].wait()
    wy[2].wait_recv()
    for p in late:
        down_x(p).start()
    wr[1].wait_recv()
    last_up()

    base = full // 2
    inner = (z == 1) | (z == 2)
    outer = (z == 0) | (z == 3)

    def sib_sum(t, p):
        return remote(
            X.at[block_rows(t), spots(p)], SR.at[block_rows(t), spots(p)], c_sib.at[t, p], to_sib
        )

    def y_sum(p):
        return remote(X.at[block_rows(1), spots(p, base)], YR.at[:, spots(p)], c_y.at[p], to_y)

    def y_early(p):
        return remote(
            X.at[own_unit(1, z), spots(p, base)], YR.at[pl.ds(0, own_rows), spots(p)],
            c_y.at[p], to_y,
        )

    def z_early(p, dz):
        to = lax.rem(z + dz, nz)
        return remote(
            X.at[own_unit(1, to), spots(p, base)], ZQ.at[dz - 1, :, spots(p)],
            c_q.at[p, dz - 1], at_z(to),
        )

    def z_sum(p, dz):
        to = lax.rem(z + dz, nz)
        return remote(
            X.at[own_unit(0, to), spots(p, base)],
            ZR.at[pl.ds((dz - 1) * own_rows, own_rows), spots(p)], c_z.at[p, dz - 1], at_z(to),
        )

    def z_in(p):
        first = jnp.where(z == 0, 1, 0)
        return remote(
            X.at[own_unit(0, first, 3), spots(p, base)],
            ZR.at[pl.ds(0, 3 * own_rows), spots(p)], c_z.at[p, 0],
            at_z(jnp.where(z == 0, 1, 2)),
        )

    def z_out(p):
        to = jnp.where(z == 1, 0, 3)
        return remote(
            X.at[own_unit(0, to), spots(p, base)],
            ZR.at[pl.ds(0, own_rows), spots(p)], c_z.at[p, 1], at_z(to),
        )

    def z_far(p, step):
        to = jnp.where(z == 1, 2, 1) if step == 1 else jnp.where(z == 1, 3, 0)
        return remote(
            X.at[own_unit(0, to), spots(p, base)],
            ZR.at[pl.ds(3 * own_rows, own_rows), spots(p)], c_z.at[p, 1 + step], at_z(to),
        )

    def strips(t):
        start = (y if t == 0 else 1 - y) * rows
        return lambda i: pl.ds(pl.multiple_of(start + i * strip, strip), strip)

    def step_a(t, p):
        @pl.loop(0, rows // strip)
        def _(i):
            r = strips(t)(i)
            X[r, spots(p)] = jnp.dot(
                H[r, :], W[:, here_cols(p, 1 - k)], preferred_element_type=jnp.float32
            ).astype(jnp.bfloat16)

        sib_sum(t, p).start()

    def step_b(t, p):
        sib_sum(t, p).wait_recv()

        @pl.loop(0, rows // strip)
        def _(i):
            r = strips(t)(i)
            X[r, spots(p, base)] = (
                jnp.dot(H[r, :], W[:, here_cols(p, k)], preferred_element_type=jnp.float32)
                + SR[r, spots(p)].astype(jnp.float32)
            ).astype(jnp.bfloat16)

        if t == 1 and p in EARLY:
            for dz in (2, 3, 1):
                z_early(p, dz).start()
        elif t == 1:
            y_sum(p).start()

    def step_q(p):
        total = X[own_unit(1, z), spots(p, base)].astype(jnp.float32)
        for dz in range(1, nz):
            z_early(p, dz).wait_recv()
            total = total + ZQ[dz - 1, :, spots(p)].astype(jnp.float32)
        X[own_unit(1, z), spots(p, base)] = total.astype(jnp.bfloat16)
        y_early(p).start()

    def step_c(p):
        if p not in EARLY:
            y_sum(p).wait_recv()

            @pl.loop(0, rows // own_rows)
            def _(i):
                r = own_unit(0, i)
                q = pl.ds(pl.multiple_of(i * own_rows, own_rows), own_rows)
                X[r, spots(p, base)] = (
                    X[r, spots(p, base)].astype(jnp.float32) + YR[q, spots(p)].astype(jnp.float32)
                ).astype(jnp.bfloat16)

        if p in DIRECT:
            for dz in (2, 3, 1):
                z_sum(p, dz).start()
        else:
            @pl.when(outer)
            def _():
                z_in(p).start()

            @pl.when(inner)
            def _():
                z_out(p).start()

    def step_d(p):
        if p not in DIRECT:
            @pl.when(inner)
            def _():
                z_in(p).wait_recv()
                r = own_unit(0, jnp.where(z == 1, 2, 0), 2)
                q = pl.ds(pl.multiple_of(jnp.where(z == 1, own_rows, 0), own_rows), 2 * own_rows)
                X[r, spots(p, base)] = (
                    X[r, spots(p, base)].astype(jnp.float32) + ZR[q, spots(p)].astype(jnp.float32)
                ).astype(jnp.bfloat16)
                z_far(p, 2).start()
                z_far(p, 1).start()

    def step_e(p):
        total = R[:, spots(p)] + X[own_unit(0, z), spots(p, base)].astype(jnp.float32)
        if p in EARLY:
            y_early(p).wait_recv()
            total = total + YR[pl.ds(0, own_rows), spots(p)].astype(jnp.float32)
        if p in DIRECT:
            for dz in range(1, nz):
                z_sum(p, dz).wait_recv()
                total = total + ZR[pl.ds((dz - 1) * own_rows, own_rows), spots(p)].astype(
                    jnp.float32
                )
        else:
            @pl.when(outer)
            def _():
                z_out(p).wait_recv()
                z_far(p, 2).wait_recv()

            @pl.when(inner)
            def _():
                z_far(p, 1).wait_recv()

            q = pl.ds(
                pl.multiple_of(jnp.where(z == 2, 2 * own_rows, 0), own_rows), own_rows
            )
            total = total + ZR[q, spots(p)].astype(jnp.float32)
            total = total + ZR[pl.ds(3 * own_rows, own_rows), spots(p)].astype(jnp.float32)
        R[:, spots(p)] = total

    bits = hash_ref.shape[1]
    side = bits // 2

    def fetch(q, p):
        return pltpu.make_async_copy(
            hash_ref.at[here_cols(p, k), pl.ds(q * side, side)],
            G.at[spots(p, q * base), pl.ds(0, side)],
            h_sem.at[q, p],
        )

    def swap(buf, sems):
        return remote(buf.at[0], buf.at[1], sems, to_sib)

    chips = lax.axis_size("batch") * nz
    me = b * nz + z
    docs = own_rows // DOC_LEN

    def tell(far):
        to = lax.rem(me + far, chips)
        return pltpu.make_async_remote_copy(
            src_ref=CA.at[me], dst_ref=CA.at[me],
            send_sem=a_send.at[far - 1], recv_sem=a_recv.at[far - 1],
            device_id={"batch": to // nz, "corpus": to % nz * 2 + k},
            device_id_type=pl.DeviceIdType.MESH,
        )

    def heard(far):
        src = lax.rem(me + chips - far, chips)
        return pltpu.make_async_remote_copy(
            src_ref=CA.at[src], dst_ref=CA.at[src],
            send_sem=a_send.at[far - 1], recv_sem=a_recv.at[far - 1],
            device_id={"batch": src // nz, "corpus": src % nz * 2 + k},
            device_id_type=pl.DeviceIdType.MESH,
        )

    def finish():
        square = jnp.sum(R[...] * R[...], axis=1, keepdims=True)
        SQ[0] = jnp.broadcast_to(square, SQ.shape[1:])
        swap(SQ, q_sem).start()
        swap(SQ, q_sem).wait()
        scale = lax.rsqrt((square + SQ[1][:, :1]) / float(full) + 1e-06)
        pooled = []
        for p in range(len(pieces)):
            final = R[:, spots(p)] * scale * last_ref[:, here_cols(p, k)]
            pooled.append(
                jnp.concatenate(
                    [
                        jnp.mean(final[d * DOC_LEN : (d + 1) * DOC_LEN], axis=0, keepdims=True)
                        for d in range(docs)
                    ]
                    + [jnp.zeros((16 - docs, pieces[p][2]), jnp.float32)],
                    axis=0,
                ).astype(jnp.bfloat16)
            )
        pooled = jnp.concatenate(pooled, axis=1)
        for q in range(2):
            for p in range(len(pieces)):
                fetch(q, p).wait()
            PT[0, :, pl.ds(q * side, side)] = jnp.dot(
                pooled, G[pl.ds(q * base, base), pl.ds(0, side)],
                preferred_element_type=jnp.float32,
            )[: PT.shape[1]]
        swap(PT, p_sem).start()
        swap(PT, p_sem).wait()
        codes = jnp.tanh(PT[0] + PT[1])[:docs]
        lanes = CA.shape[2]
        CA[me] = jnp.concatenate(
            [codes[:, g * lanes : (g + 1) * lanes] for g in range(bits // lanes)], axis=0
        ).astype(jnp.bfloat16)

        @pl.loop(1, chips)
        def _(far):
            tell(far).start()

    for act in [act for line in PLAN for act in line.split()]:
        if act == "r":
            rest()
            continue
        if act == "t":
            relay(0, nz - 2)
            continue
        if act == "hash":
            wr[0].wait_send()
            wr[1].wait_send()
            for q in range(2):
                for p in range(len(pieces)):
                    fetch(q, p).start()
            continue
        kind, p = act[0], int(act[1:])
        if kind == "w":
            down_x(p).wait_recv()
        elif kind == "a":
            step_a(1, p)
        elif kind == "A":
            step_a(0, p)
        elif kind == "b":
            step_b(1, p)
        elif kind == "B":
            step_b(0, p)
        elif kind == "q":
            step_q(p)
        elif kind == "c":
            step_c(p)
        elif kind == "d":
            step_d(p)
        elif kind == "o":
            own_product(p, p + 1)
        else:
            step_e(p)
    finish()
    for p in range(len(pieces)):
        sib_sum(0, p).wait_send()
        sib_sum(1, p).wait_send()
        if p in EARLY:
            y_early(p).wait_send()
            for dz in range(1, nz):
                z_early(p, dz).wait_send()
        else:
            y_sum(p).wait_send()
        if p in DIRECT:
            for dz in range(1, nz):
                z_sum(p, dz).wait_send()
            continue

        @pl.when(outer)
        def _(p=p):
            z_in(p).wait_send()

        @pl.when(inner)
        def _(p=p):
            z_out(p).wait_send()
            z_far(p, 1).wait_send()
            z_far(p, 2).wait_send()

    y_states.wait_send()
    for p in late:
        down_x(p).wait_send()
    for m in range(2):
        wx[m].wait_send()
    for m in range(3):
        wy[m].wait_send()

    @pl.loop(1, chips)
    def _(far):
        heard(far).wait_recv()

    @pl.loop(1, chips)
    def _(far):
        tell(far).wait_send()

    out_ref[...] = CA[...]


def wide(states, norm_gain, gate_weight, up_weight, down_weight, final_gain, hash_weight):
    nz = lax.axis_size("corpus") // 2
    rows, feat = states.shape
    full = norm_gain.shape[0]
    half = gate_weight.shape[1] // 2
    cols = down_weight.shape[1]
    w = cols // 2
    own_rows = rows // nz
    bits = hash_weight.shape[1]
    chips = lax.axis_size("batch") * nz
    packed = own_rows // DOC_LEN * (bits // 128)
    pieces = pieces_of(w)
    count = len(pieces)
    early = sum(pieces[p][2] for p in EARLY)
    dma = pltpu.SemaphoreType.DMA
    any_spec = pl.BlockSpec(memory_space=pl.ANY)
    vmem = pl.BlockSpec(memory_space=pltpu.VMEM)
    return pl.pallas_call(
        wide_kernel,
        out_shape=jax.ShapeDtypeStruct((chips, packed, 128), jnp.bfloat16),
        in_specs=[any_spec, vmem, any_spec, any_spec, any_spec, vmem, any_spec],
        out_specs=vmem,
        scratch_shapes=[
            pltpu.VMEM((2 * rows, full), jnp.bfloat16),
            pltpu.VMEM((full, half), jnp.bfloat16),
            pltpu.VMEM((full, half), jnp.bfloat16),
            pltpu.VMEM((half, full), jnp.bfloat16),
            pltpu.VMEM((rows, half), jnp.float32),
            pltpu.VMEM((rows, half), jnp.float32),
            pltpu.VMEM((2 * rows, half), jnp.bfloat16),
            pltpu.VMEM((2 * rows, full // 2), jnp.bfloat16),
            pltpu.VMEM((rows, full // 2), jnp.bfloat16),
            pltpu.VMEM((rows, full // 2), jnp.bfloat16),
            pltpu.VMEM((nz - 1, own_rows, early), jnp.bfloat16),
            pltpu.VMEM((own_rows, full // 2), jnp.float32),
            pltpu.VMEM((2, own_rows, 128), jnp.float32),
            pltpu.VMEM((2, 8, bits), jnp.float32),
            pltpu.VMEM((chips, packed, 128), jnp.bfloat16),
            dma, dma((2,)), dma((2, nz - 1, 2)), dma((2, nz - 1, 2)), dma((2, nz, 2)),
            dma((3,)), dma((2, 2)), dma((3, 2)), dma((2, 2)), dma((count, 2)),
            dma((2, count, 2)), dma((count, 2)), dma((count, 4, 2)),
            dma((len(EARLY), nz - 1, 2)), dma((2, count)), dma((2,)), dma((2,)), dma((chips - 1,)), dma((chips - 1,)),
        ],
        compiler_params=pltpu.CompilerParams(
            collective_id=0, has_side_effects=True, vmem_limit_bytes=67043328
        ),
    )(
        states, norm_gain[None], gate_weight, up_weight, down_weight, final_gain[None],
        hash_weight,
    )


def plain_codes(
    states, norm_gain, gate_weight, up_weight, down_weight, final_gain, hash_weight
):
    whole = lax.all_gather(states, "corpus", axis=1, tiled=True)
    normed = rms(whole.astype(jnp.float32), norm_gain).astype(jnp.bfloat16)

    def add_one(piece):
        return add_rows(normed, piece)

    gate = add_one(lax.all_gather(gate_weight, "batch", axis=0, tiled=True))
    up = add_one(lax.all_gather(up_weight, "batch", axis=0, tiled=True))
    hidden = (jax.nn.silu(gate) * up).astype(jnp.bfloat16)
    terms = jnp.dot(
        hidden,
        lax.all_gather(down_weight, "batch", axis=1, tiled=True),
        preferred_element_type=jnp.float32,
    )
    ffn = lax.psum_scatter(
        terms.astype(jnp.bfloat16), "corpus", scatter_dimension=0, tiled=True
    ).astype(jnp.float32)
    own_rows = ffn.shape[0]
    mine = lax.dynamic_slice_in_dim(whole, lax.axis_index("corpus") * own_rows, own_rows, 0)
    resid = mine.astype(jnp.float32) + ffn
    finals = rms(resid, final_gain)
    owned_docs = own_rows // DOC_LEN
    pooled = jnp.mean(finals.reshape(owned_docs, DOC_LEN, finals.shape[1]), axis=1).astype(
        jnp.bfloat16
    )
    codes = jnp.tanh(jnp.dot(pooled, hash_weight, preferred_element_type=jnp.float32)).astype(
        jnp.bfloat16
    )
    return lax.all_gather(codes, ("batch", "corpus"), axis=0, tiled=True)


def local(
    states,
    norm_gain,
    gate_weight,
    up_weight,
    down_weight,
    final_gain,
    hash_weight,
    query_bits,
    slot_map,
    query_index,
):
    corpus_count = lax.axis_size("corpus")
    devices = lax.axis_size("batch") * corpus_count
    flat_index = lax.axis_index("batch") * corpus_count + lax.axis_index("corpus")
    layer = (states, norm_gain, gate_weight, up_weight, down_weight, final_gain, hash_weight)
    if lax.axis_size("batch") == 4 and corpus_count == 8:
        gathered = wide(*layer)
    else:
        gathered = plain_codes(*layer)
    query_rows = query_bits.shape[0] // devices
    return score(query_bits, gathered, slot_map, query_index, flat_index, query_rows)


def solution(mesh):
    placed = (
        P("batch", "corpus"),
        P(),
        P("batch", "corpus"),
        P("batch", "corpus"),
        P("corpus", "batch"),
        P(),
        P(),
        P(),
        P(),
        P(),
    )
    return jax.shard_map(
        local, mesh=mesh, in_specs=placed, out_specs=P(("batch", "corpus"), None), check_vma=False
    )
```

```python
import jax
import jax.numpy as jnp
from jax import lax
from jax.experimental import pallas as pl
from jax.experimental.pallas import tpu as pltpu
from jax.sharding import PartitionSpec as P

DOC_LEN = 64

EARLY = (0,)
DIRECT = (8,)

PLAN = (
    "t a1 a2 a0",
    "b1 a3 b2 b0",
    "b3 r o0 F0",
    "F1 G0 o1 H0",
    "G1 H1 I0 c0",
    "A2 I1 c1 A3",
    "B2 B3 hash w4",
    "a4 A4 q0 b4",
    "B4 d0 c2 d1",
    "w5 a5 A5 b5",
    "B5 c3 d2 e0",
    "c4 d3 w6 a6",
    "A6 b6 B6 e1",
    "c5 d4 w7 a7",
    "A7 b7 B7 w8",
    "a8 A8 b8 B8",
    "e2 c6 d5 e3",
    "e4 c7 d6 c8",
    "d7 e5 e6 e7",
    "e8",
)


def pieces_of(w):
    full = [(j, h * w // 2, w // 2) for j in range(4) for h in range(2)]
    return full[:-1] + [(3, w // 2 + h * w // 4, w // 4) for h in range(2)]


def rms(values, gain):
    return values * lax.rsqrt(jnp.mean(values * values, axis=-1, keepdims=True) + 1e-06) * gain


def add_rows(left, piece):
    return jnp.dot(left, piece, preferred_element_type=jnp.float32)


def score_kernel(place_ref, bits_ref, codes_ref, slot_ref, index_ref, out_ref, picks):
    docs = slot_ref.shape[1]
    lanes = picks.shape[0]
    top = index_ref.shape[0]
    if len(codes_ref.shape) == 3:
        chips, packed, width = codes_ref.shape
        groups = bits_ref.shape[1] // width
        each = packed // groups
        every = codes_ref[...].astype(jnp.float32)
        codes = jnp.concatenate(
            [
                jnp.concatenate(
                    [every[n, g * each : (g + 1) * each] for n in range(chips)], axis=0
                )
                for g in range(groups)
            ],
            axis=1,
        ).astype(jnp.bfloat16)
    else:
        codes = codes_ref[...]
    entry = lax.broadcasted_iota(jnp.int32, (lanes, docs), 0)
    placing = jnp.where(entry == slot_ref[...], 1.0, 0.0).astype(jnp.bfloat16)
    corpus = jnp.dot(placing, codes, preferred_element_type=jnp.float32).astype(jnp.bfloat16)
    table = lax.dot_general(
        bits_ref[...],
        corpus,
        (((1,), (1,)), ((), ())),
        preferred_element_type=jnp.float32,
    ) * (1.0 / float(bits_ref.shape[1]) ** 0.5)
    picks[...] = jnp.zeros_like(picks)
    picks[:top, :] = index_ref[...]
    out_ref[...] = jnp.take_along_axis(table, picks[...].T, axis=1).T[:top, :]


def score(query_bits, codes, slot_map, query_index, flat_index, rows):
    docs = slot_map.shape[0]
    bits = query_bits.shape[1]
    top = query_index.shape[1]
    lanes = 128 * max(pl.cdiv(docs, 128), pl.cdiv(top, 128))
    index = query_index.T
    if rows % 128 == 0:
        index_spec = pl.BlockSpec((top, rows), lambda i, f: (0, f[0]))
    else:
        index = lax.dynamic_slice_in_dim(index, flat_index * rows, rows, 1)
        index_spec = pl.BlockSpec((top, rows), lambda i, f: (0, 0))
    out = pl.pallas_call(
        score_kernel,
        out_shape=jax.ShapeDtypeStruct((top, rows), jnp.float32),
        grid_spec=pltpu.PrefetchScalarGridSpec(
            num_scalar_prefetch=1,
            grid=(1,),
            in_specs=[
                pl.BlockSpec((rows, bits), lambda i, f: (f[0], 0)),
                pl.BlockSpec(codes.shape, lambda i, f: (0,) * codes.ndim),
                pl.BlockSpec((1, docs), lambda i, f: (0, 0)),
                index_spec,
            ],
            out_specs=pl.BlockSpec((top, rows), lambda i, f: (0, 0)),
            scratch_shapes=[pltpu.VMEM((lanes, rows), jnp.int32)],
        ),
    )(flat_index.reshape(1), query_bits, codes, slot_map[None], index)
    return out.T


def wide_kernel(
    states_ref, gain_ref, gate_ref, up_ref, down_ref, last_ref, hash_ref, out_ref,
    X, G, U, W, AG, AU, H, SR, YR, ZR, ZQ, R, SQ, PT, CA,
    s_loc, s_y, s_zr, s_zl, s_sib, w_loc, w_x, w_y, w_r, w_d, c_sib, c_y, c_z, c_q,
    h_sem, q_sem, p_sem, a_send, a_recv,
):
    nz = lax.axis_size("corpus") // 2
    b = lax.axis_index("batch")
    c = lax.axis_index("corpus")
    y, x = b // 2, b % 2
    z, k = c // 2, c % 2
    rows, feat = states_ref.shape
    half = W.shape[0]
    full = X.shape[1]
    cols = down_ref.shape[1]
    w = cols // 2
    by, bx, bd = (1 - y) * 2 + x, y * 2 + (1 - x), (1 - y) * 2 + (1 - x)
    to_y = {"batch": by}
    to_x = {"batch": bx}
    to_sib = {"corpus": z * 2 + (1 - k)}

    def at_z(other):
        return {"corpus": other * 2 + k}

    def remote(src, dst, sems, place):
        return pltpu.make_async_remote_copy(
            src_ref=src, dst_ref=dst, send_sem=sems.at[0], recv_sem=sems.at[1],
            device_id=place, device_id_type=pl.DeviceIdType.MESH,
        )

    def spot(t, zs, ks):
        block = y if t == 0 else 1 - y
        return X.at[
            pl.ds(pl.multiple_of(block * rows, rows), rows),
            pl.ds(pl.multiple_of((zs * 2 + ks) * feat, feat), feat),
        ]

    own_states = pltpu.make_async_copy(states_ref, spot(0, z, k), s_loc)
    y_states = remote(states_ref, X.at[
        pl.ds(pl.multiple_of(y * rows, rows), rows),
        pl.ds(pl.multiple_of(c * feat, feat), feat),
    ], s_y, to_y)

    def right(t, s):
        src = states_ref if t == 0 and s == 0 else spot(t, z - s, k)
        return remote(src, spot(t, z - s, k), s_zr.at[t, s], at_z(z + 1))

    def left(t, s):
        src = states_ref if t == 0 and s == 0 else spot(t, z + s, k)
        return remote(src, spot(t, z + s, k), s_zl.at[t, s], at_z(z - 1))

    def sib(t, zs):
        return remote(spot(t, zs, k), spot(t, zs, k), s_sib.at[t, zs], to_sib)

    def sib_in(t, zs):
        return remote(spot(t, zs, 1 - k), spot(t, zs, 1 - k), s_sib.at[t, zs], to_sib)

    def first(t):
        @pl.when(z + 1 < nz)
        def _():
            right(t, 0).start()

        @pl.when(z >= 1)
        def _():
            left(t, 0).start()

        sib(t, z).start()

    def relay(t, s):
        @pl.when(z - 1 - s >= 0)
        def _():
            right(t, s).wait_recv()
            if s + 1 < nz - 1:
                @pl.when(z + 1 < nz)
                def _():
                    right(t, s + 1).start()
            sib(t, z - 1 - s).start()

        @pl.when(z + 1 + s < nz)
        def _():
            left(t, s).wait_recv()
            if s + 1 < nz - 1:
                @pl.when(z >= 1)
                def _():
                    left(t, s + 1).start()
            sib(t, z + 1 + s).start()

    def part(m, mine):
        h = pl.ds(pl.multiple_of((y if mine else 1 - y) * half, half), half)
        if m == 2:
            return down_ref.at[h, :]
        return (gate_ref, up_ref)[m].at[:, h]

    def place(m, block):
        if m == 2:
            return W.at[:, pl.ds(pl.multiple_of(block * cols, cols), cols)]
        return (G, U)[m].at[pl.ds(pl.multiple_of(block * rows_w, rows_w), rows_w), :]

    rows_w = gate_ref.shape[0]
    loc = [pltpu.make_async_copy(part(m, True), place(m, b), w_loc.at[m]) for m in range(3)]
    wx = [remote(part(m, True), place(m, b), w_x.at[m], to_x) for m in range(2)]
    wy = [remote(part(m, False), place(m, b), w_y.at[m], to_y) for m in range(3)]
    wr = [remote(place(m, by), place(m, by), w_r.at[m], to_x) for m in range(2)]
    pieces = pieces_of(w)

    def down_pair(j, p):
        _, off, width = pieces[p]
        return W.at[
            :, pl.ds(pl.multiple_of(blocks[j] * cols + 2 * off, 2 * width), 2 * width)
        ]

    def down_x(p):
        src = down_pair(pieces[p][0] - 2, p)
        return remote(src, src, w_d.at[p], to_x)

    late = [p for p in range(len(pieces)) if pieces[p][0] >= 2]
    blocks = [x, 2 + x, 1 - x, 2 + (1 - x)]

    def settle(t):
        for zs in range(nz):
            sib_in(t, zs).wait_recv()
            sib(t, zs).wait_send()
        for s in range(nz - 1):
            @pl.when((z - s >= 0) & (z + 1 < nz))
            def _():
                right(t, s).wait_send()

            @pl.when((z + s < nz) & (z >= 1))
            def _():
                left(t, s).wait_send()

    gain = gain_ref[...]
    strip = min(512, rows)
    tile = min(512, rows)
    step = half // 3 if half % 384 == 0 else 128
    own_rows = R.shape[0]

    def block_rows(t):
        return pl.ds(pl.multiple_of((y if t == 0 else 1 - y) * rows, rows), rows)

    def own_unit(t, first, units=1):
        start = (y if t == 0 else 1 - y) * rows
        return pl.ds(pl.multiple_of(start + first * own_rows, own_rows), units * own_rows)

    def spots(p, shift=0):
        j, off, width = pieces[p]
        return pl.ds(shift + j * w + off, width)

    def here_cols(p, core):
        j, off, width = pieces[p]
        return pl.ds(pl.multiple_of(blocks[j] * cols + 2 * off + core * width, width), width)

    def norm(t):
        start = (y if t == 0 else 1 - y) * rows

        @pl.loop(0, rows // 32)
        def _(p):
            r = pl.ds(pl.multiple_of(start + p * 32, 32), 32)
            v = X[r, :].astype(jnp.float32)
            scale = lax.rsqrt(jnp.mean(v * v, axis=-1, keepdims=True) + 1e-06)
            X[r, :] = (v * scale * gain).astype(jnp.bfloat16)

    def block_product(block, order):
        depth = pl.ds(pl.multiple_of(block * rows_w, rows_w), rows_w)

        @pl.loop(0, rows // strip)
        def _(i):
            here = pl.ds(pl.multiple_of(i * strip, strip), strip)
            r = pl.ds(pl.multiple_of((1 - y) * rows + i * strip, strip), strip)

            @pl.loop(0, half // step)
            def _(j):
                h = pl.ds(pl.multiple_of(j * step, 128), step)
                g = jnp.dot(X[r, depth], G[depth, h], preferred_element_type=jnp.float32)
                u = jnp.dot(X[r, depth], U[depth, h], preferred_element_type=jnp.float32)
                if order > 0:
                    g = g + AG[here, h]
                    u = u + AU[here, h]
                AG[here, h] = g
                AU[here, h] = u

    def last_gate():
        depth = pl.ds(pl.multiple_of(bd * rows_w, rows_w), rows_w)

        @pl.loop(0, rows // strip)
        def _(i):
            here = pl.ds(pl.multiple_of(i * strip, strip), strip)
            r = pl.ds(pl.multiple_of((1 - y) * rows + i * strip, strip), strip)

            @pl.loop(0, half // step)
            def _(j):
                h = pl.ds(pl.multiple_of(j * step, 128), step)
                g = AG[here, h] + jnp.dot(
                    X[r, depth], G[depth, h], preferred_element_type=jnp.float32
                )
                AG[here, h] = g * jax.nn.sigmoid(g)

    def last_up():
        depth = pl.ds(pl.multiple_of(bd * rows_w, rows_w), rows_w)

        @pl.loop(0, rows // strip)
        def _(i):
            here = pl.ds(pl.multiple_of(i * strip, strip), strip)
            r = pl.ds(pl.multiple_of((1 - y) * rows + i * strip, strip), strip)

            @pl.loop(0, half // step)
            def _(j):
                h = pl.ds(pl.multiple_of(j * step, 128), step)
                u = AU[here, h] + jnp.dot(
                    X[r, depth], U[depth, h], preferred_element_type=jnp.float32
                )
                H[r, h] = (AG[here, h] * u).astype(jnp.bfloat16)

    def rest():
        settle(0)
        for p in range(len(pieces)):
            R[:, spots(p)] = X[own_unit(0, z), here_cols(p, k)].astype(jnp.float32)
        norm(0)

    def own_product(low, high):
        @pl.loop(low, high)
        def _(i):
            off = jnp.where(z < nz // 2, rows - tile - i * tile, i * tile)
            r = pl.ds(pl.multiple_of(y * rows + off, tile), tile)

            @pl.loop(0, half // step)
            def _(j):
                h = pl.ds(pl.multiple_of(j * step, 128), step)
                g = jnp.dot(X[r, :], G[:, h], preferred_element_type=jnp.float32)
                u = jnp.dot(X[r, :], U[:, h], preferred_element_type=jnp.float32)
                H[r, h] = (g * jax.nn.sigmoid(g) * u).astype(jnp.bfloat16)

    barrier = pltpu.get_barrier_semaphore()

    def greet(place):
        pl.semaphore_signal(
            barrier, inc=1, device_id=place, device_id_type=pl.DeviceIdType.MESH
        )

    greet(to_y)
    greet(to_x)
    greet(to_sib)

    @pl.when(z + 1 < nz)
    def _():
        greet(at_z(z + 1))

    @pl.when(z >= 1)
    def _():
        greet(at_z(z - 1))

    ends = jnp.where(z + 1 < nz, 1, 0) + jnp.where(z >= 1, 1, 0)
    pl.semaphore_wait(barrier, 3 + ends)

    y_states.start()
    own_states.start()
    wx[0].start()
    for m in range(3):
        wy[m].start()
    wx[1].start()
    own_states.wait()
    first(0)
    for m in range(3):
        loc[m].start()
    y_states.wait_recv()
    first(1)
    for s in range(nz - 1):
        relay(1, s)
        if s == 0:
            wy[0].wait_recv()
            wr[0].start()
    wy[1].wait_recv()
    wr[1].start()
    relay(0, 0)
    settle(1)
    norm(1)
    for s in range(1, nz - 2):
        relay(0, s)
    for m in range(2):
        loc[m].wait()
    block_product(b, 0)
    block_product(by, 1)
    for m in range(2):
        wx[m].wait_recv()
    block_product(bx, 2)
    wr[0].wait_recv()
    last_gate()
    loc[2].wait()
    wy[2].wait_recv()
    for p in late:
        down_x(p).start()
    wr[1].wait_recv()
    last_up()

    base = full // 2
    inner = (z == 1) | (z == 2)
    outer = (z == 0) | (z == 3)

    def sib_sum(t, p):
        return remote(
            X.at[block_rows(t), spots(p)], SR.at[block_rows(t), spots(p)], c_sib.at[t, p], to_sib
        )

    def y_sum(p):
        return remote(X.at[block_rows(1), spots(p, base)], YR.at[:, spots(p)], c_y.at[p], to_y)

    def y_early(p):
        return remote(
            X.at[own_unit(1, z), spots(p, base)], YR.at[pl.ds(0, own_rows), spots(p)],
            c_y.at[p], to_y,
        )

    def z_early(p, dz):
        to = lax.rem(z + dz, nz)
        return remote(
            X.at[own_unit(1, to), spots(p, base)], ZQ.at[dz - 1, :, spots(p)],
            c_q.at[p, dz - 1], at_z(to),
        )

    def z_sum(p, dz):
        to = lax.rem(z + dz, nz)
        return remote(
            X.at[own_unit(0, to), spots(p, base)],
            ZR.at[pl.ds((dz - 1) * own_rows, own_rows), spots(p)], c_z.at[p, dz - 1], at_z(to),
        )

    far_off = jnp.where(z < nz // 2, rows // 2, 0)

    def own_half(n):
        off = far_off if n == 0 else rows // 2 - far_off
        return pl.ds(pl.multiple_of(y * rows + off, rows // 2), rows // 2)

    def own_sib(p, n):
        r = own_half(n)
        return remote(X.at[r, spots(p)], SR.at[r, spots(p)], c_sib.at[2 * n, p], to_sib)

    def z_in(p, n):
        to = at_z(jnp.where(z == 0, 1, 2))
        if n == 0:
            land = jnp.where(z == 0, own_rows, 0)
            return remote(
                X.at[own_half(0), spots(p, base)],
                ZR.at[pl.ds(pl.multiple_of(land, own_rows), 2 * own_rows), spots(p)],
                c_z.at[p, 0], to,
            )
        land = jnp.where(z == 0, 0, 2 * own_rows)
        return remote(
            X.at[own_unit(0, jnp.where(z == 0, 1, 2)), spots(p, base)],
            ZR.at[pl.ds(pl.multiple_of(land, own_rows), own_rows), spots(p)],
            c_z.at[p, 4], to,
        )

    def z_out(p):
        to = jnp.where(z == 1, 0, 3)
        return remote(
            X.at[own_unit(0, to), spots(p, base)],
            ZR.at[pl.ds(0, own_rows), spots(p)], c_z.at[p, 1], at_z(to),
        )

    def z_far(p, step):
        to = jnp.where(z == 1, 2, 1) if step == 1 else jnp.where(z == 1, 3, 0)
        return remote(
            X.at[own_unit(0, to), spots(p, base)],
            ZR.at[pl.ds(3 * own_rows, own_rows), spots(p)], c_z.at[p, 1 + step], at_z(to),
        )

    def strips(t):
        start = (y if t == 0 else 1 - y) * rows
        return lambda i: pl.ds(pl.multiple_of(start + i * strip, strip), strip)

    def step_a(t, p):
        @pl.loop(0, rows // strip)
        def _(i):
            r = strips(t)(i)
            X[r, spots(p)] = jnp.dot(
                H[r, :], W[:, here_cols(p, 1 - k)], preferred_element_type=jnp.float32
            ).astype(jnp.bfloat16)

        sib_sum(t, p).start()

    def step_b(t, p):
        sib_sum(t, p).wait_recv()

        @pl.loop(0, rows // strip)
        def _(i):
            r = strips(t)(i)
            X[r, spots(p, base)] = (
                jnp.dot(H[r, :], W[:, here_cols(p, k)], preferred_element_type=jnp.float32)
                + SR[r, spots(p)].astype(jnp.float32)
            ).astype(jnp.bfloat16)

        if t == 1 and p in EARLY:
            for dz in (2, 3, 1):
                z_early(p, dz).start()
        elif t == 1:
            y_sum(p).start()

    def own_a(p, n):
        r = own_half(n)
        X[r, spots(p)] = jnp.dot(
            H[r, :], W[:, here_cols(p, 1 - k)], preferred_element_type=jnp.float32
        ).astype(jnp.bfloat16)
        own_sib(p, n).start()

    def own_b(p, n):
        own_sib(p, n).wait_recv()
        r = own_half(n)
        X[r, spots(p, base)] = (
            jnp.dot(H[r, :], W[:, here_cols(p, k)], preferred_element_type=jnp.float32)
            + SR[r, spots(p)].astype(jnp.float32)
        ).astype(jnp.bfloat16)

        if p in EARLY and n == 0:
            @pl.when(outer)
            def _():
                z_in(p, 0).start()

    def step_q(p):
        total = X[own_unit(1, z), spots(p, base)].astype(jnp.float32)
        for dz in range(1, nz):
            z_early(p, dz).wait_recv()
            total = total + ZQ[dz - 1, :, spots(p)].astype(jnp.float32)
        X[own_unit(1, z), spots(p, base)] = total.astype(jnp.bfloat16)
        y_early(p).start()

    def step_c(p):
        if p not in EARLY:
            y_sum(p).wait_recv()

            @pl.loop(0, rows // own_rows)
            def _(i):
                r = own_unit(0, i)
                q = pl.ds(pl.multiple_of(i * own_rows, own_rows), own_rows)
                X[r, spots(p, base)] = (
                    X[r, spots(p, base)].astype(jnp.float32) + YR[q, spots(p)].astype(jnp.float32)
                ).astype(jnp.bfloat16)

        if p in DIRECT:
            for dz in (2, 3, 1):
                z_sum(p, dz).start()
        else:
            @pl.when(outer)
            def _():
                if p not in EARLY:
                    z_in(p, 0).start()
                z_in(p, 1).start()

            @pl.when(inner)
            def _():
                z_out(p).start()

    def step_d(p):
        if p not in DIRECT:
            @pl.when(inner)
            def _():
                z_in(p, 0).wait_recv()
                r = own_unit(0, jnp.where(z == 1, 2, 0), 2)
                q = pl.ds(pl.multiple_of(jnp.where(z == 1, own_rows, 0), own_rows), 2 * own_rows)
                X[r, spots(p, base)] = (
                    X[r, spots(p, base)].astype(jnp.float32) + ZR[q, spots(p)].astype(jnp.float32)
                ).astype(jnp.bfloat16)
                z_far(p, 2).start()
                z_far(p, 1).start()

    def step_e(p):
        total = R[:, spots(p)] + X[own_unit(0, z), spots(p, base)].astype(jnp.float32)
        if p in EARLY:
            y_early(p).wait_recv()
            total = total + YR[pl.ds(0, own_rows), spots(p)].astype(jnp.float32)
        if p in DIRECT:
            for dz in range(1, nz):
                z_sum(p, dz).wait_recv()
                total = total + ZR[pl.ds((dz - 1) * own_rows, own_rows), spots(p)].astype(
                    jnp.float32
                )
        else:
            @pl.when(outer)
            def _():
                z_out(p).wait_recv()
                z_far(p, 2).wait_recv()

            @pl.when(inner)
            def _():
                z_in(p, 1).wait_recv()
                z_far(p, 1).wait_recv()

            q = pl.ds(
                pl.multiple_of(jnp.where(z == 2, 2 * own_rows, 0), own_rows), own_rows
            )
            total = total + ZR[q, spots(p)].astype(jnp.float32)
            total = total + ZR[pl.ds(3 * own_rows, own_rows), spots(p)].astype(jnp.float32)
        R[:, spots(p)] = total

    bits = hash_ref.shape[1]
    side = bits // 2

    def fetch(q, p):
        return pltpu.make_async_copy(
            hash_ref.at[here_cols(p, k), pl.ds(q * side, side)],
            G.at[spots(p, q * base), pl.ds(0, side)],
            h_sem.at[q, p],
        )

    def swap(buf, sems):
        return remote(buf.at[0], buf.at[1], sems, to_sib)

    chips = lax.axis_size("batch") * nz
    me = b * nz + z
    docs = own_rows // DOC_LEN

    def tell(far):
        to = lax.rem(me + far, chips)
        return pltpu.make_async_remote_copy(
            src_ref=CA.at[me], dst_ref=CA.at[me],
            send_sem=a_send.at[far - 1], recv_sem=a_recv.at[far - 1],
            device_id={"batch": to // nz, "corpus": to % nz * 2 + k},
            device_id_type=pl.DeviceIdType.MESH,
        )

    def heard(far):
        src = lax.rem(me + chips - far, chips)
        return pltpu.make_async_remote_copy(
            src_ref=CA.at[src], dst_ref=CA.at[src],
            send_sem=a_send.at[far - 1], recv_sem=a_recv.at[far - 1],
            device_id={"batch": src // nz, "corpus": src % nz * 2 + k},
            device_id_type=pl.DeviceIdType.MESH,
        )

    def finish():
        square = jnp.sum(R[...] * R[...], axis=1, keepdims=True)
        SQ[0] = jnp.broadcast_to(square, SQ.shape[1:])
        swap(SQ, q_sem).start()
        swap(SQ, q_sem).wait()
        scale = lax.rsqrt((square + SQ[1][:, :1]) / float(full) + 1e-06)
        pooled = []
        for p in range(len(pieces)):
            final = R[:, spots(p)] * scale * last_ref[:, here_cols(p, k)]
            pooled.append(
                jnp.concatenate(
                    [
                        jnp.mean(final[d * DOC_LEN : (d + 1) * DOC_LEN], axis=0, keepdims=True)
                        for d in range(docs)
                    ]
                    + [jnp.zeros((16 - docs, pieces[p][2]), jnp.float32)],
                    axis=0,
                ).astype(jnp.bfloat16)
            )
        pooled = jnp.concatenate(pooled, axis=1)
        for q in range(2):
            for p in range(len(pieces)):
                fetch(q, p).wait()
            PT[0, :, pl.ds(q * side, side)] = jnp.dot(
                pooled, G[pl.ds(q * base, base), pl.ds(0, side)],
                preferred_element_type=jnp.float32,
            )[: PT.shape[1]]
        swap(PT, p_sem).start()
        swap(PT, p_sem).wait()
        codes = jnp.tanh(PT[0] + PT[1])[:docs]
        lanes = CA.shape[2]
        CA[me] = jnp.concatenate(
            [codes[:, g * lanes : (g + 1) * lanes] for g in range(bits // lanes)], axis=0
        ).astype(jnp.bfloat16)

        @pl.loop(1, chips)
        def _(far):
            tell(far).start()

    for act in [act for line in PLAN for act in line.split()]:
        if act == "r":
            rest()
            continue
        if act == "t":
            relay(0, nz - 2)
            continue
        if act == "hash":
            wr[0].wait_send()
            wr[1].wait_send()
            for q in range(2):
                for p in range(len(pieces)):
                    fetch(q, p).start()
            continue
        kind, p = act[0], int(act[1:])
        if kind == "w":
            down_x(p).wait_recv()
        elif kind == "a":
            step_a(1, p)
        elif kind == "A":
            own_a(p, 0)
            own_a(p, 1)
        elif kind == "b":
            step_b(1, p)
        elif kind == "B":
            own_b(p, 0)
            own_b(p, 1)
        elif kind == "F":
            own_a(p, 0)
        elif kind == "G":
            own_b(p, 0)
        elif kind == "H":
            own_a(p, 1)
        elif kind == "I":
            own_b(p, 1)
        elif kind == "q":
            step_q(p)
        elif kind == "c":
            step_c(p)
        elif kind == "d":
            step_d(p)
        elif kind == "o":
            own_product(p, p + 1)
        else:
            step_e(p)
    finish()
    for p in range(len(pieces)):
        own_sib(p, 0).wait_send()
        own_sib(p, 1).wait_send()
        sib_sum(1, p).wait_send()
        if p in EARLY:
            y_early(p).wait_send()
            for dz in range(1, nz):
                z_early(p, dz).wait_send()
        else:
            y_sum(p).wait_send()
        if p in DIRECT:
            for dz in range(1, nz):
                z_sum(p, dz).wait_send()
            continue

        @pl.when(outer)
        def _(p=p):
            z_in(p, 0).wait_send()
            z_in(p, 1).wait_send()

        @pl.when(inner)
        def _(p=p):
            z_out(p).wait_send()
            z_far(p, 1).wait_send()
            z_far(p, 2).wait_send()

    y_states.wait_send()
    for p in late:
        down_x(p).wait_send()
    for m in range(2):
        wx[m].wait_send()
    for m in range(3):
        wy[m].wait_send()

    @pl.loop(1, chips)
    def _(far):
        heard(far).wait_recv()

    @pl.loop(1, chips)
    def _(far):
        tell(far).wait_send()

    out_ref[...] = CA[...]


def wide(states, norm_gain, gate_weight, up_weight, down_weight, final_gain, hash_weight):
    nz = lax.axis_size("corpus") // 2
    rows, feat = states.shape
    full = norm_gain.shape[0]
    half = gate_weight.shape[1] // 2
    cols = down_weight.shape[1]
    w = cols // 2
    own_rows = rows // nz
    bits = hash_weight.shape[1]
    chips = lax.axis_size("batch") * nz
    packed = own_rows // DOC_LEN * (bits // 128)
    pieces = pieces_of(w)
    count = len(pieces)
    early = sum(pieces[p][2] for p in EARLY)
    dma = pltpu.SemaphoreType.DMA
    any_spec = pl.BlockSpec(memory_space=pl.ANY)
    vmem = pl.BlockSpec(memory_space=pltpu.VMEM)
    return pl.pallas_call(
        wide_kernel,
        out_shape=jax.ShapeDtypeStruct((chips, packed, 128), jnp.bfloat16),
        in_specs=[any_spec, vmem, any_spec, any_spec, any_spec, vmem, any_spec],
        out_specs=vmem,
        scratch_shapes=[
            pltpu.VMEM((2 * rows, full), jnp.bfloat16),
            pltpu.VMEM((full, half), jnp.bfloat16),
            pltpu.VMEM((full, half), jnp.bfloat16),
            pltpu.VMEM((half, full), jnp.bfloat16),
            pltpu.VMEM((rows, half), jnp.float32),
            pltpu.VMEM((rows, half), jnp.float32),
            pltpu.VMEM((2 * rows, half), jnp.bfloat16),
            pltpu.VMEM((2 * rows, full // 2), jnp.bfloat16),
            pltpu.VMEM((rows, full // 2), jnp.bfloat16),
            pltpu.VMEM((rows, full // 2), jnp.bfloat16),
            pltpu.VMEM((nz - 1, own_rows, early), jnp.bfloat16),
            pltpu.VMEM((own_rows, full // 2), jnp.float32),
            pltpu.VMEM((2, own_rows, 128), jnp.float32),
            pltpu.VMEM((2, 8, bits), jnp.float32),
            pltpu.VMEM((chips, packed, 128), jnp.bfloat16),
            dma, dma((2,)), dma((2, nz - 1, 2)), dma((2, nz - 1, 2)), dma((2, nz, 2)),
            dma((3,)), dma((2, 2)), dma((3, 2)), dma((2, 2)), dma((count, 2)),
            dma((3, count, 2)), dma((count, 2)), dma((count, 5, 2)),
            dma((len(EARLY), nz - 1, 2)), dma((2, count)), dma((2,)), dma((2,)), dma((chips - 1,)), dma((chips - 1,)),
        ],
        compiler_params=pltpu.CompilerParams(
            collective_id=0, has_side_effects=True, vmem_limit_bytes=67043328
        ),
    )(
        states, norm_gain[None], gate_weight, up_weight, down_weight, final_gain[None],
        hash_weight,
    )


def plain_codes(
    states, norm_gain, gate_weight, up_weight, down_weight, final_gain, hash_weight
):
    whole = lax.all_gather(states, "corpus", axis=1, tiled=True)
    normed = rms(whole.astype(jnp.float32), norm_gain).astype(jnp.bfloat16)

    def add_one(piece):
        return add_rows(normed, piece)

    gate = add_one(lax.all_gather(gate_weight, "batch", axis=0, tiled=True))
    up = add_one(lax.all_gather(up_weight, "batch", axis=0, tiled=True))
    hidden = (jax.nn.silu(gate) * up).astype(jnp.bfloat16)
    terms = jnp.dot(
        hidden,
        lax.all_gather(down_weight, "batch", axis=1, tiled=True),
        preferred_element_type=jnp.float32,
    )
    ffn = lax.psum_scatter(
        terms.astype(jnp.bfloat16), "corpus", scatter_dimension=0, tiled=True
    ).astype(jnp.float32)
    own_rows = ffn.shape[0]
    mine = lax.dynamic_slice_in_dim(whole, lax.axis_index("corpus") * own_rows, own_rows, 0)
    resid = mine.astype(jnp.float32) + ffn
    finals = rms(resid, final_gain)
    owned_docs = own_rows // DOC_LEN
    pooled = jnp.mean(finals.reshape(owned_docs, DOC_LEN, finals.shape[1]), axis=1).astype(
        jnp.bfloat16
    )
    codes = jnp.tanh(jnp.dot(pooled, hash_weight, preferred_element_type=jnp.float32)).astype(
        jnp.bfloat16
    )
    return lax.all_gather(codes, ("batch", "corpus"), axis=0, tiled=True)


def local(
    states,
    norm_gain,
    gate_weight,
    up_weight,
    down_weight,
    final_gain,
    hash_weight,
    query_bits,
    slot_map,
    query_index,
):
    corpus_count = lax.axis_size("corpus")
    devices = lax.axis_size("batch") * corpus_count
    flat_index = lax.axis_index("batch") * corpus_count + lax.axis_index("corpus")
    layer = (states, norm_gain, gate_weight, up_weight, down_weight, final_gain, hash_weight)
    if lax.axis_size("batch") == 4 and corpus_count == 8:
        gathered = wide(*layer)
    else:
        gathered = plain_codes(*layer)
    query_rows = query_bits.shape[0] // devices
    return score(query_bits, gathered, slot_map, query_index, flat_index, query_rows)


def solution(mesh):
    placed = (
        P("batch", "corpus"),
        P(),
        P("batch", "corpus"),
        P("batch", "corpus"),
        P("corpus", "batch"),
        P(),
        P(),
        P(),
        P(),
        P(),
    )
    return jax.shard_map(
        local, mesh=mesh, in_specs=placed, out_specs=P(("batch", "corpus"), None), check_vma=False
    )
```

```python
import jax
import jax.numpy as jnp
from jax import lax
from jax.experimental import pallas as pl
from jax.experimental.pallas import tpu as pltpu
from jax.sharding import PartitionSpec as P

DOC_LEN = 64

EARLY = (0,)
DIRECT = ()

PLAN = (
    "t a1 a2 a0",
    "b1 a3 b2 b0",
    "b3 r o0 F0",
    "F1 G0 o1 H0",
    "G1 H1 I0 c0",
    "A2 I1 c1 A3",
    "B2 B3 hash w4",
    "a4 A4 q0 b4",
    "B4 d0 c2 d1",
    "w5 a5 A5 b5",
    "B5 c3 d2 e0",
    "c4 d3 w6 a6",
    "A6 b6 B6 e1",
    "c5 d4 w7 a7",
    "A7 b7 B7 w8",
    "a8 A8 b8 B8",
    "c6 d5 e2 e3",
    "c7 d6 e4 c8",
    "d7 e5 d8 e6",
    "e7 e8",
)


def pieces_of(w):
    full = [(j, h * w // 2, w // 2) for j in range(4) for h in range(2)]
    return full[:-1] + [(3, w // 2 + h * w // 4, w // 4) for h in range(2)]


def rms(values, gain):
    return values * lax.rsqrt(jnp.mean(values * values, axis=-1, keepdims=True) + 1e-06) * gain


def add_rows(left, piece):
    return jnp.dot(left, piece, preferred_element_type=jnp.float32)


def score_kernel(place_ref, bits_ref, codes_ref, slot_ref, index_ref, out_ref, picks):
    docs = slot_ref.shape[1]
    lanes = picks.shape[0]
    top = index_ref.shape[0]
    if len(codes_ref.shape) == 3:
        chips, packed, width = codes_ref.shape
        groups = bits_ref.shape[1] // width
        each = packed // groups
        every = codes_ref[...].astype(jnp.float32)
        codes = jnp.concatenate(
            [
                jnp.concatenate(
                    [every[n, g * each : (g + 1) * each] for n in range(chips)], axis=0
                )
                for g in range(groups)
            ],
            axis=1,
        ).astype(jnp.bfloat16)
    else:
        codes = codes_ref[...]
    entry = lax.broadcasted_iota(jnp.int32, (lanes, docs), 0)
    placing = jnp.where(entry == slot_ref[...], 1.0, 0.0).astype(jnp.bfloat16)
    corpus = jnp.dot(placing, codes, preferred_element_type=jnp.float32).astype(jnp.bfloat16)
    table = lax.dot_general(
        bits_ref[...],
        corpus,
        (((1,), (1,)), ((), ())),
        preferred_element_type=jnp.float32,
    ) * (1.0 / float(bits_ref.shape[1]) ** 0.5)
    picks[...] = jnp.zeros_like(picks)
    picks[:top, :] = index_ref[...]
    out_ref[...] = jnp.take_along_axis(table, picks[...].T, axis=1).T[:top, :]


def score(query_bits, codes, slot_map, query_index, flat_index, rows):
    docs = slot_map.shape[0]
    bits = query_bits.shape[1]
    top = query_index.shape[1]
    lanes = 128 * max(pl.cdiv(docs, 128), pl.cdiv(top, 128))
    index = query_index.T
    if rows % 128 == 0:
        index_spec = pl.BlockSpec((top, rows), lambda i, f: (0, f[0]))
    else:
        index = lax.dynamic_slice_in_dim(index, flat_index * rows, rows, 1)
        index_spec = pl.BlockSpec((top, rows), lambda i, f: (0, 0))
    out = pl.pallas_call(
        score_kernel,
        out_shape=jax.ShapeDtypeStruct((top, rows), jnp.float32),
        grid_spec=pltpu.PrefetchScalarGridSpec(
            num_scalar_prefetch=1,
            grid=(1,),
            in_specs=[
                pl.BlockSpec((rows, bits), lambda i, f: (f[0], 0)),
                pl.BlockSpec(codes.shape, lambda i, f: (0,) * codes.ndim),
                pl.BlockSpec((1, docs), lambda i, f: (0, 0)),
                index_spec,
            ],
            out_specs=pl.BlockSpec((top, rows), lambda i, f: (0, 0)),
            scratch_shapes=[pltpu.VMEM((lanes, rows), jnp.int32)],
        ),
    )(flat_index.reshape(1), query_bits, codes, slot_map[None], index)
    return out.T


def wide_kernel(
    states_ref, gain_ref, gate_ref, up_ref, down_ref, last_ref, hash_ref, out_ref,
    X, G, U, W, AG, AU, H, SR, YR, ZR, ZQ, R, SQ, PT, CA,
    s_loc, s_y, s_zr, s_zl, s_sib, w_loc, w_x, w_y, w_r, w_d, c_sib, c_y, c_z, c_q,
    h_sem, q_sem, p_sem, a_send, a_recv,
):
    nz = lax.axis_size("corpus") // 2
    b = lax.axis_index("batch")
    c = lax.axis_index("corpus")
    y, x = b // 2, b % 2
    z, k = c // 2, c % 2
    rows, feat = states_ref.shape
    half = W.shape[0]
    full = X.shape[1]
    cols = down_ref.shape[1]
    w = cols // 2
    by, bx, bd = (1 - y) * 2 + x, y * 2 + (1 - x), (1 - y) * 2 + (1 - x)
    to_y = {"batch": by}
    to_x = {"batch": bx}
    to_sib = {"corpus": z * 2 + (1 - k)}

    def at_z(other):
        return {"corpus": other * 2 + k}

    def remote(src, dst, sems, place):
        return pltpu.make_async_remote_copy(
            src_ref=src, dst_ref=dst, send_sem=sems.at[0], recv_sem=sems.at[1],
            device_id=place, device_id_type=pl.DeviceIdType.MESH,
        )

    def spot(t, zs, ks):
        block = y if t == 0 else 1 - y
        return X.at[
            pl.ds(pl.multiple_of(block * rows, rows), rows),
            pl.ds(pl.multiple_of((zs * 2 + ks) * feat, feat), feat),
        ]

    own_states = pltpu.make_async_copy(states_ref, spot(0, z, k), s_loc)
    y_states = remote(states_ref, X.at[
        pl.ds(pl.multiple_of(y * rows, rows), rows),
        pl.ds(pl.multiple_of(c * feat, feat), feat),
    ], s_y, to_y)

    def right(t, s):
        src = states_ref if t == 0 and s == 0 else spot(t, z - s, k)
        return remote(src, spot(t, z - s, k), s_zr.at[t, s], at_z(z + 1))

    def left(t, s):
        src = states_ref if t == 0 and s == 0 else spot(t, z + s, k)
        return remote(src, spot(t, z + s, k), s_zl.at[t, s], at_z(z - 1))

    def sib(t, zs):
        return remote(spot(t, zs, k), spot(t, zs, k), s_sib.at[t, zs], to_sib)

    def sib_in(t, zs):
        return remote(spot(t, zs, 1 - k), spot(t, zs, 1 - k), s_sib.at[t, zs], to_sib)

    def first(t):
        @pl.when(z + 1 < nz)
        def _():
            right(t, 0).start()

        @pl.when(z >= 1)
        def _():
            left(t, 0).start()

        sib(t, z).start()

    def relay(t, s):
        @pl.when(z - 1 - s >= 0)
        def _():
            right(t, s).wait_recv()
            if s + 1 < nz - 1:
                @pl.when(z + 1 < nz)
                def _():
                    right(t, s + 1).start()
            sib(t, z - 1 - s).start()

        @pl.when(z + 1 + s < nz)
        def _():
            left(t, s).wait_recv()
            if s + 1 < nz - 1:
                @pl.when(z >= 1)
                def _():
                    left(t, s + 1).start()
            sib(t, z + 1 + s).start()

    def part(m, mine):
        h = pl.ds(pl.multiple_of((y if mine else 1 - y) * half, half), half)
        if m == 2:
            return down_ref.at[h, :]
        return (gate_ref, up_ref)[m].at[:, h]

    def place(m, block):
        if m == 2:
            return W.at[:, pl.ds(pl.multiple_of(block * cols, cols), cols)]
        return (G, U)[m].at[pl.ds(pl.multiple_of(block * rows_w, rows_w), rows_w), :]

    rows_w = gate_ref.shape[0]
    loc = [pltpu.make_async_copy(part(m, True), place(m, b), w_loc.at[m]) for m in range(3)]
    wx = [remote(part(m, True), place(m, b), w_x.at[m], to_x) for m in range(2)]
    wy = [remote(part(m, False), place(m, b), w_y.at[m], to_y) for m in range(3)]
    wr = [remote(place(m, by), place(m, by), w_r.at[m], to_x) for m in range(2)]
    pieces = pieces_of(w)

    def down_pair(j, p):
        _, off, width = pieces[p]
        return W.at[
            :, pl.ds(pl.multiple_of(blocks[j] * cols + 2 * off, 2 * width), 2 * width)
        ]

    def down_x(p):
        src = down_pair(pieces[p][0] - 2, p)
        return remote(src, src, w_d.at[p], to_x)

    late = [p for p in range(len(pieces)) if pieces[p][0] >= 2]
    blocks = [x, 2 + x, 1 - x, 2 + (1 - x)]

    def settle(t):
        for zs in range(nz):
            sib_in(t, zs).wait_recv()
            sib(t, zs).wait_send()
        for s in range(nz - 1):
            @pl.when((z - s >= 0) & (z + 1 < nz))
            def _():
                right(t, s).wait_send()

            @pl.when((z + s < nz) & (z >= 1))
            def _():
                left(t, s).wait_send()

    gain = gain_ref[...]
    strip = min(512, rows)
    tile = min(512, rows)
    step = half // 3 if half % 384 == 0 else 128
    own_rows = R.shape[0]

    def block_rows(t):
        return pl.ds(pl.multiple_of((y if t == 0 else 1 - y) * rows, rows), rows)

    def own_unit(t, first, units=1):
        start = (y if t == 0 else 1 - y) * rows
        return pl.ds(pl.multiple_of(start + first * own_rows, own_rows), units * own_rows)

    def spots(p, shift=0):
        j, off, width = pieces[p]
        return pl.ds(shift + j * w + off, width)

    def here_cols(p, core):
        j, off, width = pieces[p]
        return pl.ds(pl.multiple_of(blocks[j] * cols + 2 * off + core * width, width), width)

    def norm(t):
        start = (y if t == 0 else 1 - y) * rows

        @pl.loop(0, rows // 32)
        def _(p):
            r = pl.ds(pl.multiple_of(start + p * 32, 32), 32)
            v = X[r, :].astype(jnp.float32)
            scale = lax.rsqrt(jnp.mean(v * v, axis=-1, keepdims=True) + 1e-06)
            X[r, :] = (v * scale * gain).astype(jnp.bfloat16)

    def block_product(block, order):
        depth = pl.ds(pl.multiple_of(block * rows_w, rows_w), rows_w)

        @pl.loop(0, rows // strip)
        def _(i):
            here = pl.ds(pl.multiple_of(i * strip, strip), strip)
            r = pl.ds(pl.multiple_of((1 - y) * rows + i * strip, strip), strip)

            @pl.loop(0, half // step)
            def _(j):
                h = pl.ds(pl.multiple_of(j * step, 128), step)
                g = jnp.dot(X[r, depth], G[depth, h], preferred_element_type=jnp.float32)
                u = jnp.dot(X[r, depth], U[depth, h], preferred_element_type=jnp.float32)
                if order > 0:
                    g = g + AG[here, h]
                    u = u + AU[here, h]
                AG[here, h] = g
                AU[here, h] = u

    def last_gate():
        depth = pl.ds(pl.multiple_of(bd * rows_w, rows_w), rows_w)

        @pl.loop(0, rows // strip)
        def _(i):
            here = pl.ds(pl.multiple_of(i * strip, strip), strip)
            r = pl.ds(pl.multiple_of((1 - y) * rows + i * strip, strip), strip)

            @pl.loop(0, half // step)
            def _(j):
                h = pl.ds(pl.multiple_of(j * step, 128), step)
                g = AG[here, h] + jnp.dot(
                    X[r, depth], G[depth, h], preferred_element_type=jnp.float32
                )
                AG[here, h] = g * jax.nn.sigmoid(g)

    def last_up():
        depth = pl.ds(pl.multiple_of(bd * rows_w, rows_w), rows_w)

        @pl.loop(0, rows // strip)
        def _(i):
            here = pl.ds(pl.multiple_of(i * strip, strip), strip)
            r = pl.ds(pl.multiple_of((1 - y) * rows + i * strip, strip), strip)

            @pl.loop(0, half // step)
            def _(j):
                h = pl.ds(pl.multiple_of(j * step, 128), step)
                u = AU[here, h] + jnp.dot(
                    X[r, depth], U[depth, h], preferred_element_type=jnp.float32
                )
                H[r, h] = (AG[here, h] * u).astype(jnp.bfloat16)

    def rest():
        settle(0)
        for p in range(len(pieces)):
            R[:, spots(p)] = X[own_unit(0, z), here_cols(p, k)].astype(jnp.float32)
        norm(0)

    def own_product(low, high):
        @pl.loop(low, high)
        def _(i):
            off = jnp.where(z < nz // 2, rows - tile - i * tile, i * tile)
            r = pl.ds(pl.multiple_of(y * rows + off, tile), tile)

            @pl.loop(0, half // step)
            def _(j):
                h = pl.ds(pl.multiple_of(j * step, 128), step)
                g = jnp.dot(X[r, :], G[:, h], preferred_element_type=jnp.float32)
                u = jnp.dot(X[r, :], U[:, h], preferred_element_type=jnp.float32)
                H[r, h] = (g * jax.nn.sigmoid(g) * u).astype(jnp.bfloat16)

    barrier = pltpu.get_barrier_semaphore()

    def greet(place):
        pl.semaphore_signal(
            barrier, inc=1, device_id=place, device_id_type=pl.DeviceIdType.MESH
        )

    greet(to_y)
    greet(to_x)
    greet(to_sib)

    @pl.when(z + 1 < nz)
    def _():
        greet(at_z(z + 1))

    @pl.when(z >= 1)
    def _():
        greet(at_z(z - 1))

    ends = jnp.where(z + 1 < nz, 1, 0) + jnp.where(z >= 1, 1, 0)
    pl.semaphore_wait(barrier, 3 + ends)

    y_states.start()
    own_states.start()
    wx[0].start()
    for m in range(3):
        wy[m].start()
    wx[1].start()
    own_states.wait()
    first(0)
    for m in range(3):
        loc[m].start()
    y_states.wait_recv()
    first(1)
    for s in range(nz - 1):
        relay(1, s)
        if s == 0:
            wy[0].wait_recv()
            wr[0].start()
    wy[1].wait_recv()
    wr[1].start()
    relay(0, 0)
    settle(1)
    norm(1)
    for s in range(1, nz - 2):
        relay(0, s)
    for m in range(2):
        loc[m].wait()
    block_product(b, 0)
    block_product(by, 1)
    for m in range(2):
        wx[m].wait_recv()
    block_product(bx, 2)
    wr[0].wait_recv()
    last_gate()
    loc[2].wait()
    wy[2].wait_recv()
    for p in late:
        down_x(p).start()
    wr[1].wait_recv()
    last_up()

    base = full // 2
    inner = (z == 1) | (z == 2)
    outer = (z == 0) | (z == 3)

    def sib_sum(t, p):
        return remote(
            X.at[block_rows(t), spots(p)], SR.at[block_rows(t), spots(p)], c_sib.at[t, p], to_sib
        )

    def y_sum(p):
        return remote(X.at[block_rows(1), spots(p, base)], YR.at[:, spots(p)], c_y.at[p], to_y)

    def y_early(p):
        return remote(
            X.at[own_unit(1, z), spots(p, base)], YR.at[pl.ds(0, own_rows), spots(p)],
            c_y.at[p], to_y,
        )

    def z_early(p, dz):
        to = lax.rem(z + dz, nz)
        return remote(
            X.at[own_unit(1, to), spots(p, base)], ZQ.at[dz - 1, :, spots(p)],
            c_q.at[p, dz - 1], at_z(to),
        )

    def z_sum(p, dz):
        to = lax.rem(z + dz, nz)
        return remote(
            X.at[own_unit(0, to), spots(p, base)],
            ZR.at[pl.ds((dz - 1) * own_rows, own_rows), spots(p)], c_z.at[p, dz - 1], at_z(to),
        )

    far_off = jnp.where(z < nz // 2, rows // 2, 0)

    def own_half(n):
        off = far_off if n == 0 else rows // 2 - far_off
        return pl.ds(pl.multiple_of(y * rows + off, rows // 2), rows // 2)

    def own_sib(p, n):
        r = own_half(n)
        return remote(X.at[r, spots(p)], SR.at[r, spots(p)], c_sib.at[2 * n, p], to_sib)

    def z_in(p, n):
        to = at_z(jnp.where(z == 0, 1, 2))
        if n == 0:
            land = jnp.where(z == 0, own_rows, 0)
            return remote(
                X.at[own_half(0), spots(p, base)],
                ZR.at[pl.ds(pl.multiple_of(land, own_rows), 2 * own_rows), spots(p)],
                c_z.at[p, 0], to,
            )
        land = jnp.where(z == 0, 0, 2 * own_rows)
        return remote(
            X.at[own_unit(0, jnp.where(z == 0, 1, 2)), spots(p, base)],
            ZR.at[pl.ds(pl.multiple_of(land, own_rows), own_rows), spots(p)],
            c_z.at[p, 4], to,
        )

    def z_out(p):
        to = jnp.where(z == 1, 0, 3)
        return remote(
            X.at[own_unit(0, to), spots(p, base)],
            ZR.at[pl.ds(0, own_rows), spots(p)], c_z.at[p, 1], at_z(to),
        )

    def z_far(p, step):
        to = jnp.where(z == 1, 2, 1) if step == 1 else jnp.where(z == 1, 3, 0)
        return remote(
            X.at[own_unit(0, to), spots(p, base)],
            ZR.at[pl.ds(3 * own_rows, own_rows), spots(p)], c_z.at[p, 1 + step], at_z(to),
        )

    def strips(t):
        start = (y if t == 0 else 1 - y) * rows
        return lambda i: pl.ds(pl.multiple_of(start + i * strip, strip), strip)

    def step_a(t, p):
        @pl.loop(0, rows // strip)
        def _(i):
            r = strips(t)(i)
            X[r, spots(p)] = jnp.dot(
                H[r, :], W[:, here_cols(p, 1 - k)], preferred_element_type=jnp.float32
            ).astype(jnp.bfloat16)

        sib_sum(t, p).start()

    def step_b(t, p):
        sib_sum(t, p).wait_recv()

        @pl.loop(0, rows // strip)
        def _(i):
            r = strips(t)(i)
            X[r, spots(p, base)] = (
                jnp.dot(H[r, :], W[:, here_cols(p, k)], preferred_element_type=jnp.float32)
                + SR[r, spots(p)].astype(jnp.float32)
            ).astype(jnp.bfloat16)

        if t == 1 and p in EARLY:
            for dz in (2, 3, 1):
                z_early(p, dz).start()
        elif t == 1:
            y_sum(p).start()

    def own_a(p, n):
        r = own_half(n)
        X[r, spots(p)] = jnp.dot(
            H[r, :], W[:, here_cols(p, 1 - k)], preferred_element_type=jnp.float32
        ).astype(jnp.bfloat16)
        own_sib(p, n).start()

    def own_b(p, n):
        own_sib(p, n).wait_recv()
        r = own_half(n)
        X[r, spots(p, base)] = (
            jnp.dot(H[r, :], W[:, here_cols(p, k)], preferred_element_type=jnp.float32)
            + SR[r, spots(p)].astype(jnp.float32)
        ).astype(jnp.bfloat16)

        if p in EARLY and n == 0:
            @pl.when(outer)
            def _():
                z_in(p, 0).start()

    def step_q(p):
        total = X[own_unit(1, z), spots(p, base)].astype(jnp.float32)
        for dz in range(1, nz):
            z_early(p, dz).wait_recv()
            total = total + ZQ[dz - 1, :, spots(p)].astype(jnp.float32)
        X[own_unit(1, z), spots(p, base)] = total.astype(jnp.bfloat16)
        y_early(p).start()

    def step_c(p):
        if p not in EARLY:
            y_sum(p).wait_recv()

            for n in range(2):
                off = far_off if n == 0 else rows // 2 - far_off

                @pl.loop(0, rows // 2 // own_rows)
                def _(i, off=off):
                    here = off + i * own_rows
                    r = pl.ds(pl.multiple_of(y * rows + here, own_rows), own_rows)
                    q = pl.ds(pl.multiple_of(here, own_rows), own_rows)
                    X[r, spots(p, base)] = (
                        X[r, spots(p, base)].astype(jnp.float32)
                        + YR[q, spots(p)].astype(jnp.float32)
                    ).astype(jnp.bfloat16)

                if n == 0 and p not in DIRECT:
                    @pl.when(outer)
                    def _():
                        z_in(p, 0).start()

        if p in DIRECT:
            for dz in (2, 3, 1):
                z_sum(p, dz).start()
        else:
            @pl.when(outer)
            def _():
                z_in(p, 1).start()

            @pl.when(inner)
            def _():
                z_out(p).start()

    def step_d(p):
        if p not in DIRECT:
            @pl.when(inner)
            def _():
                z_in(p, 0).wait_recv()
                r = own_unit(0, jnp.where(z == 1, 2, 0), 2)
                q = pl.ds(pl.multiple_of(jnp.where(z == 1, own_rows, 0), own_rows), 2 * own_rows)
                X[r, spots(p, base)] = (
                    X[r, spots(p, base)].astype(jnp.float32) + ZR[q, spots(p)].astype(jnp.float32)
                ).astype(jnp.bfloat16)
                z_far(p, 2).start()
                z_far(p, 1).start()

    def step_e(p):
        total = R[:, spots(p)] + X[own_unit(0, z), spots(p, base)].astype(jnp.float32)
        if p in EARLY:
            y_early(p).wait_recv()
            total = total + YR[pl.ds(0, own_rows), spots(p)].astype(jnp.float32)
        if p in DIRECT:
            for dz in range(1, nz):
                z_sum(p, dz).wait_recv()
                total = total + ZR[pl.ds((dz - 1) * own_rows, own_rows), spots(p)].astype(
                    jnp.float32
                )
        else:
            @pl.when(outer)
            def _():
                z_out(p).wait_recv()
                z_far(p, 2).wait_recv()

            @pl.when(inner)
            def _():
                z_in(p, 1).wait_recv()
                z_far(p, 1).wait_recv()

            q = pl.ds(
                pl.multiple_of(jnp.where(z == 2, 2 * own_rows, 0), own_rows), own_rows
            )
            total = total + ZR[q, spots(p)].astype(jnp.float32)
            total = total + ZR[pl.ds(3 * own_rows, own_rows), spots(p)].astype(jnp.float32)
        R[:, spots(p)] = total

    bits = hash_ref.shape[1]
    side = bits // 2

    def fetch(q, p):
        return pltpu.make_async_copy(
            hash_ref.at[here_cols(p, k), pl.ds(q * side, side)],
            G.at[spots(p, q * base), pl.ds(0, side)],
            h_sem.at[q, p],
        )

    def swap(buf, sems):
        return remote(buf.at[0], buf.at[1], sems, to_sib)

    chips = lax.axis_size("batch") * nz
    me = b * nz + z
    docs = own_rows // DOC_LEN

    def tell(far):
        to = lax.rem(me + far, chips)
        return pltpu.make_async_remote_copy(
            src_ref=CA.at[me], dst_ref=CA.at[me],
            send_sem=a_send.at[far - 1], recv_sem=a_recv.at[far - 1],
            device_id={"batch": to // nz, "corpus": to % nz * 2 + k},
            device_id_type=pl.DeviceIdType.MESH,
        )

    def heard(far):
        src = lax.rem(me + chips - far, chips)
        return pltpu.make_async_remote_copy(
            src_ref=CA.at[src], dst_ref=CA.at[src],
            send_sem=a_send.at[far - 1], recv_sem=a_recv.at[far - 1],
            device_id={"batch": src // nz, "corpus": src % nz * 2 + k},
            device_id_type=pl.DeviceIdType.MESH,
        )

    def finish():
        square = jnp.sum(R[...] * R[...], axis=1, keepdims=True)
        SQ[0] = jnp.broadcast_to(square, SQ.shape[1:])
        swap(SQ, q_sem).start()
        swap(SQ, q_sem).wait()
        scale = lax.rsqrt((square + SQ[1][:, :1]) / float(full) + 1e-06)
        pooled = []
        for p in range(len(pieces)):
            final = R[:, spots(p)] * scale * last_ref[:, here_cols(p, k)]
            pooled.append(
                jnp.concatenate(
                    [
                        jnp.mean(final[d * DOC_LEN : (d + 1) * DOC_LEN], axis=0, keepdims=True)
                        for d in range(docs)
                    ]
                    + [jnp.zeros((16 - docs, pieces[p][2]), jnp.float32)],
                    axis=0,
                ).astype(jnp.bfloat16)
            )
        pooled = jnp.concatenate(pooled, axis=1)
        for q in range(2):
            for p in range(len(pieces)):
                fetch(q, p).wait()
            PT[0, :, pl.ds(q * side, side)] = jnp.dot(
                pooled, G[pl.ds(q * base, base), pl.ds(0, side)],
                preferred_element_type=jnp.float32,
            )[: PT.shape[1]]
        swap(PT, p_sem).start()
        swap(PT, p_sem).wait()
        codes = jnp.tanh(PT[0] + PT[1])[:docs]
        lanes = CA.shape[2]
        CA[me] = jnp.concatenate(
            [codes[:, g * lanes : (g + 1) * lanes] for g in range(bits // lanes)], axis=0
        ).astype(jnp.bfloat16)

        @pl.loop(1, chips)
        def _(far):
            tell(far).start()

    for act in [act for line in PLAN for act in line.split()]:
        if act == "r":
            rest()
            continue
        if act == "t":
            relay(0, nz - 2)
            continue
        if act == "hash":
            wr[0].wait_send()
            wr[1].wait_send()
            for q in range(2):
                for p in range(len(pieces)):
                    fetch(q, p).start()
            continue
        kind, p = act[0], int(act[1:])
        if kind == "w":
            down_x(p).wait_recv()
        elif kind == "a":
            step_a(1, p)
        elif kind == "A":
            own_a(p, 0)
            own_a(p, 1)
        elif kind == "b":
            step_b(1, p)
        elif kind == "B":
            own_b(p, 0)
            own_b(p, 1)
        elif kind == "F":
            own_a(p, 0)
        elif kind == "G":
            own_b(p, 0)
        elif kind == "H":
            own_a(p, 1)
        elif kind == "I":
            own_b(p, 1)
        elif kind == "q":
            step_q(p)
        elif kind == "c":
            step_c(p)
        elif kind == "d":
            step_d(p)
        elif kind == "o":
            own_product(p, p + 1)
        else:
            step_e(p)
    finish()
    for p in range(len(pieces)):
        own_sib(p, 0).wait_send()
        own_sib(p, 1).wait_send()
        sib_sum(1, p).wait_send()
        if p in EARLY:
            y_early(p).wait_send()
            for dz in range(1, nz):
                z_early(p, dz).wait_send()
        else:
            y_sum(p).wait_send()
        if p in DIRECT:
            for dz in range(1, nz):
                z_sum(p, dz).wait_send()
            continue

        @pl.when(outer)
        def _(p=p):
            z_in(p, 0).wait_send()
            z_in(p, 1).wait_send()

        @pl.when(inner)
        def _(p=p):
            z_out(p).wait_send()
            z_far(p, 1).wait_send()
            z_far(p, 2).wait_send()

    y_states.wait_send()
    for p in late:
        down_x(p).wait_send()
    for m in range(2):
        wx[m].wait_send()
    for m in range(3):
        wy[m].wait_send()

    @pl.loop(1, chips)
    def _(far):
        heard(far).wait_recv()

    @pl.loop(1, chips)
    def _(far):
        tell(far).wait_send()

    out_ref[...] = CA[...]


def wide(states, norm_gain, gate_weight, up_weight, down_weight, final_gain, hash_weight):
    nz = lax.axis_size("corpus") // 2
    rows, feat = states.shape
    full = norm_gain.shape[0]
    half = gate_weight.shape[1] // 2
    cols = down_weight.shape[1]
    w = cols // 2
    own_rows = rows // nz
    bits = hash_weight.shape[1]
    chips = lax.axis_size("batch") * nz
    packed = own_rows // DOC_LEN * (bits // 128)
    pieces = pieces_of(w)
    count = len(pieces)
    early = sum(pieces[p][2] for p in EARLY)
    dma = pltpu.SemaphoreType.DMA
    any_spec = pl.BlockSpec(memory_space=pl.ANY)
    vmem = pl.BlockSpec(memory_space=pltpu.VMEM)
    return pl.pallas_call(
        wide_kernel,
        out_shape=jax.ShapeDtypeStruct((chips, packed, 128), jnp.bfloat16),
        in_specs=[any_spec, vmem, any_spec, any_spec, any_spec, vmem, any_spec],
        out_specs=vmem,
        scratch_shapes=[
            pltpu.VMEM((2 * rows, full), jnp.bfloat16),
            pltpu.VMEM((full, half), jnp.bfloat16),
            pltpu.VMEM((full, half), jnp.bfloat16),
            pltpu.VMEM((half, full), jnp.bfloat16),
            pltpu.VMEM((rows, half), jnp.float32),
            pltpu.VMEM((rows, half), jnp.float32),
            pltpu.VMEM((2 * rows, half), jnp.bfloat16),
            pltpu.VMEM((2 * rows, full // 2), jnp.bfloat16),
            pltpu.VMEM((rows, full // 2), jnp.bfloat16),
            pltpu.VMEM((rows, full // 2), jnp.bfloat16),
            pltpu.VMEM((nz - 1, own_rows, early), jnp.bfloat16),
            pltpu.VMEM((own_rows, full // 2), jnp.float32),
            pltpu.VMEM((2, own_rows, 128), jnp.float32),
            pltpu.VMEM((2, 8, bits), jnp.float32),
            pltpu.VMEM((chips, packed, 128), jnp.bfloat16),
            dma, dma((2,)), dma((2, nz - 1, 2)), dma((2, nz - 1, 2)), dma((2, nz, 2)),
            dma((3,)), dma((2, 2)), dma((3, 2)), dma((2, 2)), dma((count, 2)),
            dma((3, count, 2)), dma((count, 2)), dma((count, 5, 2)),
            dma((len(EARLY), nz - 1, 2)), dma((2, count)), dma((2,)), dma((2,)), dma((chips - 1,)), dma((chips - 1,)),
        ],
        compiler_params=pltpu.CompilerParams(
            collective_id=0, has_side_effects=True, vmem_limit_bytes=67043328
        ),
    )(
        states, norm_gain[None], gate_weight, up_weight, down_weight, final_gain[None],
        hash_weight,
    )


def plain_codes(
    states, norm_gain, gate_weight, up_weight, down_weight, final_gain, hash_weight
):
    whole = lax.all_gather(states, "corpus", axis=1, tiled=True)
    normed = rms(whole.astype(jnp.float32), norm_gain).astype(jnp.bfloat16)

    def add_one(piece):
        return add_rows(normed, piece)

    gate = add_one(lax.all_gather(gate_weight, "batch", axis=0, tiled=True))
    up = add_one(lax.all_gather(up_weight, "batch", axis=0, tiled=True))
    hidden = (jax.nn.silu(gate) * up).astype(jnp.bfloat16)
    terms = jnp.dot(
        hidden,
        lax.all_gather(down_weight, "batch", axis=1, tiled=True),
        preferred_element_type=jnp.float32,
    )
    ffn = lax.psum_scatter(
        terms.astype(jnp.bfloat16), "corpus", scatter_dimension=0, tiled=True
    ).astype(jnp.float32)
    own_rows = ffn.shape[0]
    mine = lax.dynamic_slice_in_dim(whole, lax.axis_index("corpus") * own_rows, own_rows, 0)
    resid = mine.astype(jnp.float32) + ffn
    finals = rms(resid, final_gain)
    owned_docs = own_rows // DOC_LEN
    pooled = jnp.mean(finals.reshape(owned_docs, DOC_LEN, finals.shape[1]), axis=1).astype(
        jnp.bfloat16
    )
    codes = jnp.tanh(jnp.dot(pooled, hash_weight, preferred_element_type=jnp.float32)).astype(
        jnp.bfloat16
    )
    return lax.all_gather(codes, ("batch", "corpus"), axis=0, tiled=True)


def local(
    states,
    norm_gain,
    gate_weight,
    up_weight,
    down_weight,
    final_gain,
    hash_weight,
    query_bits,
    slot_map,
    query_index,
):
    corpus_count = lax.axis_size("corpus")
    devices = lax.axis_size("batch") * corpus_count
    flat_index = lax.axis_index("batch") * corpus_count + lax.axis_index("corpus")
    layer = (states, norm_gain, gate_weight, up_weight, down_weight, final_gain, hash_weight)
    if lax.axis_size("batch") == 4 and corpus_count == 8:
        gathered = wide(*layer)
    else:
        gathered = plain_codes(*layer)
    query_rows = query_bits.shape[0] // devices
    return score(query_bits, gathered, slot_map, query_index, flat_index, query_rows)


def solution(mesh):
    placed = (
        P("batch", "corpus"),
        P(),
        P("batch", "corpus"),
        P("batch", "corpus"),
        P("corpus", "batch"),
        P(),
        P(),
        P(),
        P(),
        P(),
    )
    return jax.shard_map(
        local, mesh=mesh, in_specs=placed, out_specs=P(("batch", "corpus"), None), check_vma=False
    )
```
